32 devices in a mesh: ens: 2 (over x), lon: 16 (over z, y, core).
Axes of the slice: x: 2, y: 2, z: 4, core: 2. Of those that a mesh axis runs over, the one named last changes fastest.
Arguments:
- tracer: float32 [4, 256, 75, 256], P(None, 'lon', None, 'ens'), parts along dimension 3, may hold values from -6 to 6
- east_speed: float32 [256, 75, 256], P('lon', None, 'ens'), parts along dimension 2, may hold values from -0.25 to 0.25
- north_speed: float32 [256, 75, 256], P('lon', None, 'ens'), parts along dimension 2, may hold values from -0.25 to 0.25
- diffusivity: float32 [256, 75, 256], P('lon', None, 'ens'), parts along dimension 2, may hold values from 0.02 to 0.2
- mixing: float32 [256, 75, 256], P('lon', None, 'ens'), parts along dimension 2, may hold values from 0.05 to 5
- thickness: float32 [256, 75, 256], P('lon', None, 'ens'), parts along dimension 2, may hold values from 0.5 to 2
- depth_levels: int32 [256, 256], P('lon', 'ens'), parts along dimension 1, may hold values from 0 to 75
- air_flux: float32 [8, 4096], P('ens', 'lon'), parts along dimension 0, may hold values from -6 to 6
- margin_tile: int32 [32768, 1], P(('ens', 'lon')), parts along dimension 0, may hold values from 0 to 15; in each aligned block of 1024 rows (0 to 1023, 1024 to 2047, ...) at most 64 rows name the same one
- margin_source: int32 [32768], P(('ens', 'lon')), parts along dimension 0, may hold values from 0 to 255
- margin_cell: int32 [32768], P(('ens', 'lon')), parts along dimension 0, may hold values from 0 to 2047
- margin_weight: float32 [32768], P(('ens', 'lon')), parts along dimension 0, may hold values from 0.2 to 1
Outputs:
- tracer_next: float32 [4, 256, 75, 256], P(None, 'lon', None, 'ens'), parts along dimension 3
The draws below stay inside these ranges and needn't reach their ends.
There are 2 independent parts, one for each index of `ens`. The reference program is written for one: setup_inputs(seed, part) draws one part's arguments, and reference() takes and returns one part's arrays. A program takes and returns all parts, laid end to end along the dimension named above; each array names one. Nothing has to cross between parts.
Inputs may be any that keep to these rules, and one draw needn't show every extreme that they name: `margin_tile`: the rows of one tile name each ocean tile at most 64 times.
All inputs are finite; a program needn't handle non-finite values.
Results may differ from the reference program's by a relative error of at most 0.00002.
Values sent between devices are 32-bit elements; how exact they have to be, the bound alone decides.
A program may use at most 192 MiB of HBM per device.

```python
import math
import jax
import jax.numpy as jnp
import numpy as np

LX = 16
NY = 128
NZ = 75
TRACERS = 4
ACELL_DEV = 256
OVL_DEV = 1024
CAP = 64
NX = 256
ACELLS = 4096
OVL = 16384
N_LON = 16


def touch_ends(entries, own_key, least, top_value):
    shape = entries.shape
    place = [jax.random.randint(jax.random.fold_in(own_key, axis), (), 0, shape[axis]) for axis in range(len(shape))]
    entries = entries.at[tuple(place)].set(least)
    longest = shape.index(max(shape))
    place[longest] = (place[longest] + 1) % shape[longest]
    return entries.at[tuple(place)].set(top_value)


def block_scale(key, extent, cuts, least, high):
    loudness, own = 1.0, jax.random.fold_in(key, 6)
    for position, parts in cuts:
        draws = jnp.exp(jax.random.uniform(jax.random.fold_in(own, position), (parts,), jnp.float32, least / len(cuts), high / len(cuts)))
        loudness = loudness * jnp.repeat(draws, extent[position] // parts).reshape([-1 if axis == position else 1 for axis in range(len(extent))])
    return loudness


def shared_out(key, own, number, rows, amount, top, bound, lean):
    ranking = jax.random.permutation(key, amount)
    heavy_load, ordinary = portions_of(amount, rows * top, bound, lean, True), portions_of(amount, rows * top, bound, lean, False)
    places = jnp.arange(amount)

    def named(lengths, rotation):
        used = int((lengths > 0).sum())
        fixed = max(1, used // 4)
        shifted = fixed + (places - fixed + rotation * (used - fixed)) % max(1, amount - fixed)
        return jnp.zeros((amount,), jnp.int32).at[ranking[jnp.where(places < fixed, places, shifted)]].set(jnp.asarray(lengths, jnp.int32))

    lengths = jnp.where(number % 4 == 0, named(heavy_load, number // 4), named(ordinary, number - number // 4 - 1))
    mixed = jax.random.permutation(jax.random.fold_in(own, 3), amount)
    giver, sink = mixed[0:amount // 2 * 2:2], mixed[1:amount // 2 * 2:2]
    margin = jnp.minimum(lengths[giver] - 1, bound - lengths[sink]) // 2
    margin = jnp.where((giver == ranking[0]) | (sink == ranking[0]) | (lengths[sink] == 0), 0, jnp.maximum(margin, 0))
    shifted = jax.random.randint(jax.random.fold_in(own, 4), (amount // 2,), 0, 1 << 20) % (margin + 1)
    lengths = lengths.at[giver].add(-shifted).at[sink].add(shifted)
    items = jnp.searchsorted(jnp.cumsum(lengths), jnp.arange(rows * top), side="right").astype(jnp.int32)
    listing = items.reshape(top, rows).T
    listing = listing[jax.random.permutation(jax.random.fold_in(own, 1), rows)]
    rotation = jax.random.randint(jax.random.fold_in(own, 2), (rows, 1), 0, top)
    return jnp.take_along_axis(listing, (jnp.arange(top)[None, :] + rotation) % top, axis=1)


def portions_of(number_of, total, most, slope, full):
    loads = [(1 << 20) // math.isqrt(rank ** slope) + 1 for rank in range(1, number_of + 1)]
    largest = most if full else min(most, max(-(-total // number_of), total * loads[0] // sum(loads)))
    least = 1 if total - largest >= number_of - 1 else 0
    given, surplus = [largest] + [least] * (number_of - 1), total - largest - least * (number_of - 1)
    while surplus > 0:
        candidates = [i for i in range(1, number_of) if given[i] < largest] or [i for i in range(1, number_of) if given[i] < most]
        pool, left = sum([loads[i] for i in candidates]), surplus
        for i in candidates:
            extra = min(most - given[i], max(1, left * loads[i] // pool), surplus)
            given[i] = given[i] + extra
            surplus = surplus - extra
    return np.array(given)


def bell_draw(own_key, dims, deviation, most, pieces=(), kind=jnp.bfloat16):
    result = deviation * jax.random.normal(own_key, dims, jnp.float32)
    if pieces:
        result = result * block_scale(own_key, dims, pieces, -0.22, 0.18)
    return jnp.clip(result, -most, most).astype(kind)


def setup_inputs(seed: int = 0, part: int = 0) -> dict:
    keys = jax.random.split(jax.random.key(seed), 13)
    own_keys = jax.random.split(jax.random.fold_in(keys[12], part), 13)
    tracer = bell_draw(own_keys[0], (TRACERS, NX, NZ, NY), 1.0, 6.0, ((1, 16),), jnp.float32)
    east_speed = jnp.clip(jax.random.uniform(own_keys[1], (NX, NZ, NY), jnp.float32, -0.25, 0.25) * block_scale(own_keys[1], (NX, NZ, NY), ((0, 16),), -0.4, 0.0), -0.25, 0.25)
    north_speed = jnp.clip(jax.random.uniform(own_keys[2], (NX, NZ, NY), jnp.float32, -0.25, 0.25) * block_scale(own_keys[2], (NX, NZ, NY), ((0, 16),), -0.4, 0.0), -0.25, 0.25)
    diffusivity = jnp.clip(jnp.exp(math.log(0.2) - 2.3025851 * jax.random.uniform(own_keys[3], (NX, NZ, NY), jnp.float32) ** block_scale(own_keys[3], (NX, NZ, NY), ((0, 16),), -0.2, 0.2)), 0.02, 0.2)
    mixing = jnp.clip(jnp.exp(math.log(5.0) - 4.6051702 * jax.random.uniform(own_keys[4], (NX, NZ, NY), jnp.float32) ** block_scale(own_keys[4], (NX, NZ, NY), ((0, 16),), -0.2, 0.2)), 0.05, 5.0)
    thickness = jnp.clip(jnp.exp(math.log(2.0) - 1.3862944 * jax.random.uniform(own_keys[5], (NX, NZ, NY), jnp.float32) ** block_scale(own_keys[5], (NX, NZ, NY), ((0, 16),), -0.2, 0.2)), 0.5, 2.0)
    depth_levels = touch_ends(jax.random.randint(own_keys[6], (NX, NY), 0, NZ + 1), jax.random.fold_in(own_keys[6], 1), 0, NZ).astype(jnp.int32)
    air_flux = bell_draw(own_keys[7], (TRACERS, ACELLS), 1.0, 6.0, ((1, 16),), jnp.float32)
    margin_tile_keys = jax.random.split(jax.random.fold_in(own_keys[8], 1), OVL // OVL_DEV)
    margin_tile_turns = jax.random.permutation(jax.random.fold_in(own_keys[8], 3), OVL // OVL_DEV)
    margin_tile = jax.vmap(lambda own, number: shared_out(jax.random.fold_in(own_keys[8], 2), own, number, OVL_DEV, N_LON, 1, CAP, 2))(margin_tile_keys, margin_tile_turns).reshape((OVL, 1))
    margin_source = touch_ends(jax.random.randint(own_keys[9], (OVL,), 0, ACELL_DEV), jax.random.fold_in(own_keys[9], 1), 0, ACELL_DEV - 1).astype(jnp.int32)
    margin_cell = touch_ends(jax.random.randint(own_keys[10], (OVL,), 0, LX * NY), jax.random.fold_in(own_keys[10], 1), 0, (LX * NY) - 1).astype(jnp.int32)
    margin_weight = jnp.clip(0.2 + 0.8 * jax.random.uniform(own_keys[11], (OVL,), jnp.float32) ** block_scale(own_keys[11], (OVL,), ((0, 16),), -0.2, 0.2), 0.2, 1.0)
    return {"tracer": tracer, "east_speed": east_speed, "north_speed": north_speed, "diffusivity": diffusivity, "mixing": mixing, "thickness": thickness, "depth_levels": depth_levels, "air_flux": air_flux, "margin_tile": margin_tile, "margin_source": margin_source, "margin_cell": margin_cell, "margin_weight": margin_weight}


def face_flux(speed, kappa_near, kappa_far, open_face, near, far):
    return open_face * (jnp.maximum(speed, 0.0) * near + jnp.minimum(speed, 0.0) * far + 0.5 * (kappa_near + kappa_far) * (near - far))


def mix_columns(stepped, mixing, thickness, wet_mask, surface):
    levels = stepped.shape[2]
    wet_below = jnp.concatenate([wet_mask[:, 1:], jnp.zeros_like(wet_mask[:, :1])], axis=1)
    thickness_below = jnp.concatenate([thickness[:, 1:], thickness[:, -1:]], axis=1)
    coupling = mixing * wet_below / (0.5 * (thickness + thickness_below))
    prior_coupling = jnp.zeros_like(thickness[:, 0])
    prior_gain = jnp.zeros_like(thickness[:, 0])
    prior_value = jnp.zeros_like(stepped[:, :, 0])
    gain_list = []
    value_list = []
    for level_index in range(levels):
        here_coupling = coupling[:, level_index]
        here_thickness = thickness[:, level_index]
        pivot_value = here_thickness + here_coupling + prior_coupling - prior_coupling * prior_gain
        right_side = here_thickness * stepped[:, :, level_index]
        if level_index == 0:
            right_side = right_side + wet_mask[:, 0] * surface
        prior_value = (right_side + prior_coupling * prior_value) / pivot_value
        prior_gain = here_coupling / pivot_value
        prior_coupling = here_coupling
        gain_list.append(prior_gain)
        value_list.append(prior_value)
    solved = [value_list[-1]]
    for level_index in range(levels - 2, -1, -1):
        solved.append(value_list[level_index] + gain_list[level_index] * solved[-1])
    return jnp.stack(solved[::-1], axis=2)


def reference(tracer, east_speed, north_speed, diffusivity, mixing, thickness, depth_levels, air_flux, margin_tile, margin_source, margin_cell, margin_weight):
    level_ids = jnp.arange(NZ).astype(jnp.int32)
    wet_mask = (level_ids[None, :, None] < depth_levels[:, None, :]).astype(jnp.float32)
    east_flux = face_flux(east_speed[None], diffusivity[None], jnp.roll(diffusivity, -1, axis=0)[None], (wet_mask * jnp.roll(wet_mask, -1, axis=0))[None], tracer, jnp.roll(tracer, -1, axis=1))
    zonal_change = east_flux - jnp.roll(east_flux, 1, axis=1)
    mirror_tracer = jnp.flip(tracer[:, :, :, -1], axis=1)
    mirror_speed = jnp.flip(north_speed[:, :, -1], axis=0)
    mirror_kappa = jnp.flip(diffusivity[:, :, -1], axis=0)
    mirror_wet = jnp.flip(wet_mask[:, :, -1], axis=0)
    fold_flux = face_flux((0.5 * (north_speed[:, :, -1] - mirror_speed))[None], diffusivity[None, :, :, -1], mirror_kappa[None], (wet_mask[:, :, -1] * mirror_wet)[None], tracer[:, :, :, -1], mirror_tracer)
    inner_flux = face_flux(north_speed[None, :, :, :-1], diffusivity[None, :, :, :-1], diffusivity[None, :, :, 1:], (wet_mask[:, :, :-1] * wet_mask[:, :, 1:])[None], tracer[:, :, :, :-1], tracer[:, :, :, 1:])
    north_flux = jnp.concatenate([inner_flux, fold_flux[..., None]], axis=3)
    south_flux = jnp.concatenate([jnp.zeros_like(inner_flux[..., :1]), inner_flux], axis=3)
    stepped = tracer - zonal_change - (north_flux - south_flux)
    owner = (jnp.arange(OVL) // OVL_DEV).astype(jnp.int32)
    source = owner * ACELL_DEV + margin_source
    payload = margin_weight[None, :] * jnp.take(air_flux, source, axis=1)
    target = margin_tile[:, 0] * (LX * NY) + margin_cell
    surface = jnp.zeros((TRACERS, NX * NY), jnp.float32).at[:, target].add(payload).reshape(TRACERS, NX, NY)
    return mix_columns(stepped, mixing, thickness, wet_mask, surface)
```

```python
import jax
import jax.numpy as jnp
from jax import lax
from jax.experimental import pallas as pl
from jax.experimental.pallas import tpu as pltpu
from jax.sharding import PartitionSpec as P

CAP = 64
CHUNK = 8
PIECE = 30
SUB = 8
LANES = 128
F32 = jnp.float32
BF16 = jnp.bfloat16
I32 = jnp.int32


def iota(shape, axis):
    return lax.broadcasted_iota(I32, shape, axis)


def thirds(x):
    high = x.astype(BF16).astype(F32)
    rest = x - high
    middle = rest.astype(BF16).astype(F32)
    return high, middle, rest - middle


def route(tiles, tile, source, cells, weight, air, send_ref):
    count, air_cells = air.shape
    records = tile.shape[1]
    picks = (iota((air_cells, records), 0) == source).astype(F32).astype(BF16)
    parts = jnp.concatenate(thirds(air), axis=0).astype(BF16)
    found = jnp.dot(parts, picks, preferred_element_type=F32)
    found = found[:count] + (found[count:2 * count] + found[2 * count:])
    payload = weight * found

    chosen = (iota((tiles, records), 0) == tile).astype(F32)
    earlier = (iota((LANES, LANES), 0) < iota((LANES, LANES), 1)).astype(F32).astype(BF16)
    carried = jnp.zeros((tiles, 1), F32)
    slots = []
    for start in range(0, records, LANES):
        piece = chosen[:, start:start + LANES]
        rank = jnp.dot(piece.astype(BF16), earlier, preferred_element_type=F32) + carried
        slots.append(jnp.sum(piece * rank, axis=0, keepdims=True))
        carried = carried + jnp.sum(piece, axis=1, keepdims=True)
    slot = jnp.concatenate(slots, axis=1)
    places = (iota((CAP, records), 0).astype(F32) == slot).astype(F32).astype(BF16)

    row = (cells >> 7).astype(F32)
    column = (cells & (LANES - 1)).astype(F32)
    lines = [p[n:n + 1] for p in thirds(payload) for n in range(count)] + [row, column]
    spread = jnp.concatenate([(chosen * line).astype(BF16) for line in lines], axis=0)
    packed = lax.dot_general(spread, places, (((1,), (1,)), ((), ())), preferred_element_type=F32)

    def part(index):
        return packed[index * tiles:(index + 1) * tiles]

    values = [part(n) + (part(count + n) + part(2 * count + n)) for n in range(count)]
    place = part(3 * count) * LANES + part(3 * count + 1)
    for r in range(count // 2):
        send_ref[:, r, :] = jnp.concatenate(values[2 * r:2 * r + 2], axis=1)
    for r in range(count // 2, send_ref.shape[1]):
        send_ref[:, r, :] = jnp.concatenate([place, place], axis=1)


def gathered(received, count, lon_cells):
    first = iota((received.shape[1], LANES), 1) < CAP
    spread, spots = [], []
    for s in range(0, received.shape[0], 2):
        even, odd = received[s], received[s + 1]
        low = jnp.where(first, even, pltpu.roll(odd, CAP, 1))
        high = jnp.where(first, pltpu.roll(even, CAP, 1), odd)
        cell = low[count // 2:count // 2 + 1].astype(I32)
        hit = iota((lon_cells, LANES), 0) == cell >> 7
        low, high = thirds(low), thirds(high)
        lines = [(high if n % 2 else low)[p][n // 2:n // 2 + 1]
                 for p in range(3) for n in range(count)]
        spread.append(jnp.concatenate(
            [jnp.where(hit, line, 0.0).astype(BF16) for line in lines], axis=0))
        spots.append((iota((LANES, LANES), 0) == (cell & (LANES - 1))).astype(F32).astype(BF16))
    surface = jnp.zeros((3 * count * lon_cells, LANES), F32)
    for a, b in zip(spread, spots):
        surface = surface + lax.dot_general(
            a, b, (((1,), (1,)), ((), ())), preferred_element_type=F32)
    fluxes = []
    for n in range(count):
        block = [surface[(p * count + n) * lon_cells:(p * count + n + 1) * lon_cells]
                 for p in range(3)]
        fluxes.append(block[0] + (block[1] + block[2]))
    return fluxes


def weights(speed, near, far, open_face):
    half = 0.5 * (near + far)
    return (jnp.where(open_face, jnp.maximum(speed, 0.0) + half, 0.0),
            jnp.where(open_face, jnp.minimum(speed, 0.0) - half, 0.0))


def step(tiles, *refs):
    sources, (wide, kappa_wide, east_wide, depth_wide), refs = refs[:12], refs[12:16], refs[16:]
    values, gains, refs = refs[0], refs[1], refs[2:]
    held, refs = refs[:12], refs[12:]
    (factor, share, top, fold_out, fold_in, right_in, left_in, right_depth, left_depth,
     opens, send, received, load_sems, out_sems, in_sems, pair_out, pair_in, own_sem,
     near, present) = refs
    (tracer, east, north, kappa, mixing, thickness, depth_ref, air, tile, source, cells,
     weight) = held
    count, planes = tracer.shape[:2]
    lon_cells = depth_ref.shape[0]
    levels = planes // lon_cells
    last = lon_cells - 1
    spare = LANES - levels

    pieces = [(begin, min(begin + PIECE, levels)) for begin in range(0, levels, PIECE)]
    loads = {}

    def load(i, a, b):
        loads[i] = pltpu.make_async_copy(a, b, load_sems.at[len(loads)])
        loads[i].start()

    for i in (7, 8, 9, 10, 11):
        load(i, sources[i], held[i])

    me = lax.axis_index("lon")
    right = lax.rem(me + 1, tiles)
    left = lax.rem(me + tiles - 1, tiles)
    partner = tiles - 1 - me
    barrier = pltpu.get_barrier_semaphore()

    def signal(semaphore, device):
        pl.semaphore_signal(semaphore, inc=1, device_id={"lon": device},
                            device_id_type=pl.DeviceIdType.MESH)

    @pl.loop(me + 1, tiles)
    def _(other):
        signal(barrier, other)

    load(6, sources[6], held[6])
    for p, (begin, end) in enumerate(pieces):
        block = pl.ds(begin * lon_cells, (end - begin) * lon_cells)
        load((0, p), sources[0].at[:, block], tracer.at[:, block])
        for i in (3, 2):
            load((i, p), sources[i].at[block], held[i].at[block])
    for i in (5, 4, 1):
        load(i, sources[i], held[i])

    copies = []

    def copy(a, b, device):
        index = len(copies)
        copies.append(pltpu.make_async_remote_copy(
            src_ref=a, dst_ref=b, send_sem=out_sems.at[index], recv_sem=in_sems.at[index],
            device_id={"lon": device}, device_id_type=pl.DeviceIdType.MESH))
        return copies[-1]

    rows = pl.ds(0, levels)
    to_right = [
        copy(wide.at[:, :, last, 0, :], right_in.at[pl.ds(0, count), rows, :], right),
        copy(kappa_wide.at[:, last, 0, :], right_in.at[count, rows, :], right),
        copy(east_wide.at[:, last, 0, :], right_in.at[count + 1, rows, :], right),
        copy(depth_wide.at[last], right_depth, right)]
    to_left = [
        copy(wide.at[:, :, 0, 0, :], left_in.at[pl.ds(0, count), rows, :], left),
        copy(kappa_wide.at[:, 0, 0, :], left_in.at[count, rows, :], left),
        copy(depth_wide.at[0], left_depth, left)]
    to_partner = copy(fold_out, fold_in, partner)

    def start(group):
        for each in group:
            each.start()

    def pair(other, sender):
        return pltpu.make_async_remote_copy(
            src_ref=send.at[other], dst_ref=received.at[sender], send_sem=pair_out.at[other],
            recv_sem=pair_in.at[sender], device_id={"lon": other},
            device_id_type=pl.DeviceIdType.MESH)

    @pl.when(me > 0)
    def _():
        pl.semaphore_wait(barrier, me)
        signal(near.at[0], left)
        start(to_left)

    @pl.when(me == tiles - 1)
    def _():
        signal(near.at[1], right)
        start(to_right)

    @pl.when(partner < me)
    def _():
        signal(near.at[2], partner)

    @pl.loop(0, me)
    def _(other):
        signal(present.at[me], other)

    for i in (7, 8, 9, 10, 11):
        loads[i].wait()
    route(tiles, tile[...], source[...], cells[...], weight[...], air[...], send)

    @pl.loop(0, me)
    def _(other):
        pair(other, me).start()

    own = pltpu.make_async_copy(send.at[me], received.at[me], own_sem)
    own.start()

    loads[6].wait()
    depth = depth_ref[...]

    def at(k):
        return pl.ds(pl.multiple_of(k * lon_cells, lon_cells), lon_cells)

    def column(i):
        return pl.ds(i, levels, stride=lon_cells)

    lane = iota((lon_cells, LANES), 1)

    def take(k, packed):
        fields = [tracer[n, at(k), :] for n in range(count)] + [kappa[at(k), :], north[at(k), :]]
        return tuple(jnp.where(lane == k, pltpu.roll(x, k + 1, 1), p)
                     for x, p in zip(fields, packed))

    empty = jnp.zeros((lon_cells, LANES), F32)
    packed = (empty,) * (count + 2)
    for p, (begin, end) in enumerate(pieces):
        for i in (0, 3, 2):
            loads[(i, p)].wait()
        packed = lax.fori_loop(begin, end, take, packed, unroll=15)
    edge = jnp.broadcast_to(depth[:, LANES - 1:].astype(F32), (lon_cells, LANES))
    for f, plane in enumerate(packed + (edge,)):
        top[f] = plane
    sent = list(packed[:count])
    for f in range(2):
        field = packed[count + f]
        sent[2 * f] = jnp.where(lane < levels, sent[2 * f], pltpu.roll(field, levels, 1))
        sent[2 * f + 1] = jnp.where(
            lane < levels, sent[2 * f + 1], pltpu.roll(field, levels - spare, 1))
    sent[1] = jnp.where(lane == LANES - 1, edge, sent[1])
    for f, plane in enumerate(sent):
        for i in range(lon_cells):
            fold_out[f, last - i:last - i + 1, :] = plane[i:i + 1]

    @pl.when(partner < me)
    def _():
        to_partner.start()

    @pl.when(me < tiles - 1)
    def _():
        pl.semaphore_wait(near.at[0], 1)
        start(to_right)

    row = iota((lon_cells, LANES), 0)
    opens[0] = jnp.where(row == last, 0, jnp.minimum(depth, pltpu.roll(depth, last, 0)))
    opens[1] = jnp.where(
        lane == LANES - 1, 0, jnp.minimum(depth, pltpu.roll(depth, LANES - 1, 1)))
    for i in (5, 4, 1):
        loads[i].wait()

    middle = (levels + 1) // 2
    chunks = (levels + SUB - 1) // SUB
    rounds = (middle + chunks - 1) // chunks

    def eliminate(k, target, coupling, prior, rest):
        here = thickness[at(k), :]
        partial = here + rest
        scale = 1.0 / (partial + coupling)
        gain = coupling * scale
        gains[at(target), :] = gain
        factor[at(target), :] = prior * scale
        share[at(target), :] = here * scale
        return gain * partial

    def below(k):
        near_by = 0.5 * (thickness[at(k), :] + thickness[at(k + 1), :])
        return jnp.where(depth > k + 1, mixing[at(k), :] / near_by, 0.0)

    def inner(c, state):
        over, over_rest, under, under_rest = state
        for s in range(rounds):
            k = c * rounds + s
            coupling = below(k)
            over_rest = eliminate(
                k, jnp.where(k < middle, k, levels), coupling, over, over_rest)
            over = coupling
            k = levels - 1 - k
            coupling = below(k - 1)
            under_rest = eliminate(
                k, jnp.where(k >= middle, k, levels), coupling, under, under_rest)
            under = coupling

        first = jnp.minimum(c * SUB, levels - SUB)
        deep = iota((SUB, LANES), 0) + first

        def cells(i):
            return pl.ds(first * lon_cells + i, SUB, stride=lon_cells)

        spread = 0.5 * kappa[cells(0), :]
        fields = [tracer[n, cells(0), :] for n in range(count)]
        zonal = [None] * count
        for i in range(lon_cells):
            speed = north[cells(i), :]
            ahead = jnp.maximum(speed, 0.0) + (spread + pltpu.roll(spread, LANES - 1, 1))
            open_face = deep < opens[1, i:i + 1, :]
            na = jnp.where(open_face, ahead, 0.0)
            nb = jnp.where(open_face, speed - ahead, 0.0)
            if i < last:
                speed = east[cells(i), :]
                spread_next = 0.5 * kappa[cells(i + 1), :]
                ahead = jnp.maximum(speed, 0.0) + (spread + spread_next)
                open_face = deep < opens[0, i:i + 1, :]
                ea = jnp.where(open_face, ahead, 0.0)
                eb = jnp.where(open_face, speed - ahead, 0.0)
                spread = spread_next
            for n in range(count):
                t = fields[n]
                up = na * t + nb * pltpu.roll(t, LANES - 1, 1)
                stepped = t - (up - pltpu.roll(up, 1, 1))
                if i:
                    stepped = stepped + zonal[n]
                if i < last:
                    fields[n] = tracer[n, cells(i + 1), :]
                    zonal[n] = ea * t + eb * fields[n]
                    stepped = stepped - zonal[n]
                values[n, cells(i), :] = stepped
        return over, over_rest, under, under_rest

    lax.fori_loop(0, chunks, inner, (empty,) * 4)

    @pl.when(me == 0)
    def _():
        pl.semaphore_wait(near.at[1], 1)
        start(to_left)

    @pl.when(partner > me)
    def _():
        pl.semaphore_wait(near.at[2], 1)
        to_partner.start()

    @pl.loop(me + 1, tiles)
    def _(other):
        pl.semaphore_wait(present.at[other], 1)
        pair(other, me).start()

    own.wait()

    @pl.loop(1, tiles)
    def _(hop):
        other = lax.rem(me + hop, tiles)
        pair(other, other).wait_recv()

    surface = gathered(received, count, lon_cells)
    thin = 1.0 / thickness[at(0), :]
    for n in range(count):
        values[n, at(0), :] = values[n, at(0), :] + jnp.where(depth > 0, surface[n] * thin, 0.0)

    for each in copies:
        each.wait_recv()
    deep = iota((levels, LANES), 0)

    wa, wb = weights(right_in[count + 1, rows, :], right_in[count, rows, :], kappa[column(0), :],
                     deep < jnp.minimum(right_depth[...], depth[:1]))
    ea, eb = weights(east[column(last), :], kappa[column(last), :], left_in[count, rows, :],
                     deep < jnp.minimum(left_depth[...], depth[last:]))
    for n in range(count):
        flux = wa * right_in[n, rows, :] + wb * tracer[n, column(0), :]
        values[n, column(0), :] = values[n, column(0), :] + flux
        flux = ea * tracer[n, column(last), :] + eb * left_in[n, rows, :]
        values[n, column(last), :] = values[n, column(last), :] - flux
    came = [fold_in[n] for n in range(count)]
    kappa_far, north_far = [
        jnp.where(lane < spare, pltpu.roll(came[2 * f], spare, 1),
                  pltpu.roll(came[2 * f + 1], LANES - levels + spare, 1)) for f in range(2)]
    edge_far = jnp.broadcast_to(came[1][:, LANES - 1:], (lon_cells, LANES))
    fa, fb = weights(0.5 * (top[count + 1] - north_far), top[count], kappa_far,
                     lane < jnp.minimum(top[count + 2], edge_far).astype(I32))
    fold = [fa * top[n] + fb * came[n] for n in range(count)]

    def sweep(k, value):
        part = share[at(k), :]
        mult = factor[at(k), :]
        solved = []
        for n in range(count):
            across = jnp.where(lane == LANES - 1, pltpu.roll(fold[n], LANES - 1 - k, 1), 0.0)
            solved.append(part * (values[n, at(k), :] - across) + mult * value[n])
            values[n, at(k), :] = solved[n]
        return tuple(solved)

    def both(k, state):
        return sweep(k, state[:count]) + sweep(levels - 1 - k, state[count:])

    state = lax.fori_loop(0, levels // 2, both, (empty,) * (2 * count), unroll=5)
    if levels % 2:
        sweep(levels // 2, state[:count])

    for each in copies:
        each.wait_send()

    @pl.loop(1, tiles)
    def _(hop):
        other = lax.rem(me + hop, tiles)
        pair(other, other).wait_send()


def finish(lon_cells, values, gains, out, solved, sems):
    count, planes = values.shape[:2]
    levels = planes // lon_cells
    middle = (levels + 1) // 2

    def at(k):
        return pl.ds(pl.multiple_of(k * lon_cells, lon_cells), lon_cells)

    stores = []

    def store(begin, end):
        block = pl.ds(begin * lon_cells, (end - begin) * lon_cells)
        stores.append(pltpu.make_async_copy(
            solved.at[:, block], out.at[:, block], sems.at[len(stores)]))
        stores[-1].start()

    def put(k, value):
        for n in range(count):
            solved[n, at(k), :] = value[n]

    gain, other = gains[at(middle - 1), :], gains[at(middle), :]
    over = [values[n, at(middle - 1), :] for n in range(count)]
    under = [values[n, at(middle), :] for n in range(count)]
    scale = 1.0 / (1.0 - gain * other)
    over = [(a + gain * b) * scale for a, b in zip(over, under)]
    under = [b + other * a for a, b in zip(over, under)]
    put(middle - 1, over)
    put(middle, under)

    top, bottom = middle - 1, middle + 1
    while top > 0 or bottom < levels:
        size = CHUNK - 1 if not stores else CHUNK
        for k in range(top - 1, max(top - size, 0) - 1, -1):
            gain = gains[at(k), :]
            over = [values[n, at(k), :] + gain * over[n] for n in range(count)]
            put(k, over)
        for k in range(bottom, min(bottom + size, levels)):
            gain = gains[at(k), :]
            under = [values[n, at(k), :] + gain * under[n] for n in range(count)]
            put(k, under)
        low, high = max(top - size, 0), min(bottom + size, levels)
        if not stores:
            store(low, high)
        else:
            if low < top:
                store(low, top)
            if bottom < high:
                store(bottom, high)
        top, bottom = low, high
    for each in stores:
        each.wait()


def shards(tracer, east_speed, north_speed, diffusivity, mixing, thickness, depth_levels,
           air_flux, margin_tile, margin_source, margin_cell, margin_weight):
    count, lon_cells, levels, lat_cells = tracer.shape
    tiles = lax.axis_size("lon")
    records = margin_source.shape[0]
    assert lat_cells == LANES and levels < LANES

    def by_level(x):
        return x.transpose(1, 0, 2).reshape(levels * lon_cells, LANES)

    operands = (
        tracer.transpose(0, 2, 1, 3).reshape(count, levels * lon_cells, LANES),
        *[by_level(x) for x in (east_speed, north_speed, diffusivity, mixing, thickness)],
        depth_levels, air_flux,
        *[x.reshape(1, records) for x in (margin_tile, margin_source, margin_cell, margin_weight)])
    wide = (
        tracer.transpose(0, 2, 1, 3).reshape(count, levels, lon_cells, 1, LANES),
        *[x.transpose(1, 0, 2).reshape(levels, lon_cells, 1, LANES)
          for x in (diffusivity, east_speed)],
        depth_levels.reshape(lon_cells, 1, LANES))
    hbm = pl.BlockSpec(memory_space=pltpu.HBM)
    more = pltpu.VMEM(((levels + 1) * lon_cells, LANES), F32)
    rows = (levels + 7) // 8 * 8
    pairs = pltpu.VMEM((tiles, (count // 2 + 4) // 4 * 4, LANES), F32)
    dma = pltpu.SemaphoreType.DMA
    regular = pltpu.SemaphoreType.REGULAR
    vmem = pl.BlockSpec(memory_space=pltpu.VMEM)
    values, gains = pl.pallas_call(
        lambda *refs: step(tiles, *refs),
        out_shape=(pltpu.VMEM(operands[0].shape, F32), more),
        in_specs=[hbm] * 16, out_specs=(vmem, vmem),
        scratch_shapes=[pltpu.VMEM(x.shape, x.dtype) for x in operands] + [
            more, more,
            pltpu.VMEM((count + 3, lon_cells, LANES), F32),
            pltpu.VMEM((count, lon_cells, LANES), F32), pltpu.VMEM((count, lon_cells, LANES), F32),
            pltpu.VMEM((count + 2, rows, LANES), F32), pltpu.VMEM((count + 1, rows, LANES), F32),
            pltpu.VMEM((1, LANES), I32), pltpu.VMEM((1, LANES), I32),
            pltpu.VMEM((2, lon_cells, LANES), I32), pairs, pairs, dma((24,)), dma((8,)), dma((8,)),
            dma((tiles,)), dma((tiles,)), dma, regular((3,)), regular((tiles,))],
        compiler_params=pltpu.CompilerParams(
            collective_id=0, has_side_effects=True, vmem_limit_bytes=32 << 20),
        name="ocean_step",
    )(*[pltpu.with_memory_space_constraint(x, pltpu.HBM) for x in operands + wide])
    result = pl.pallas_call(
        lambda *refs: finish(lon_cells, *refs),
        out_shape=pltpu.HBM(values.shape, F32),
        in_specs=[vmem, vmem], out_specs=hbm,
        scratch_shapes=[pltpu.VMEM(values.shape, F32), dma((2 * pl.cdiv(levels, 2 * CHUNK),))],
        name="finish",
    )(*[pltpu.with_memory_space_constraint(x, pltpu.VMEM) for x in (values, gains)])
    return result.reshape(count, levels, lon_cells, LANES).transpose(0, 2, 1, 3)


def solution(mesh):
    placed = (
        P(None, "lon", None, "ens"),
        P("lon", None, "ens"),
        P("lon", None, "ens"),
        P("lon", None, "ens"),
        P("lon", None, "ens"),
        P("lon", None, "ens"),
        P("lon", "ens"),
        P("ens", "lon"),
        P(("ens", "lon"), None),
        P(("ens", "lon")),
        P(("ens", "lon")),
        P(("ens", "lon")),
    )
    return jax.shard_map(
        shards, mesh=mesh, in_specs=placed, out_specs=P(None, "lon", None, "ens"), check_vma=False
    )
```

```python
import jax
import jax.numpy as jnp
from jax import lax
from jax.experimental import pallas as pl
from jax.experimental.pallas import tpu as pltpu
from jax.sharding import PartitionSpec as P

CAP = 64
CHUNK = 8
PIECE = 30
PAD = 8
GROUP = 5
LANES = 128
F32 = jnp.float32
BF16 = jnp.bfloat16
I32 = jnp.int32


def iota(shape, axis):
    return lax.broadcasted_iota(I32, shape, axis)


def thirds(x):
    high = x.astype(BF16).astype(F32)
    rest = x - high
    middle = rest.astype(BF16).astype(F32)
    return high, middle, rest - middle


def halves(x):
    high = x.astype(BF16)
    return high, (x - high.astype(F32)).astype(BF16)


def route(tiles, tile, source, cells, weight, air, send_ref):
    count, air_cells = air.shape
    records = tile.shape[1]
    picks = (iota((air_cells, records), 0) == source).astype(F32).astype(BF16)
    parts = jnp.concatenate(thirds(air), axis=0).astype(BF16)
    found = jnp.dot(parts, picks, preferred_element_type=F32)
    found = found[:count] + (found[count:2 * count] + found[2 * count:])
    payload = weight * found

    chosen = (iota((tiles, records), 0) == tile).astype(F32)
    earlier = (iota((LANES, LANES), 0) < iota((LANES, LANES), 1)).astype(F32).astype(BF16)
    carried = jnp.zeros((tiles, 1), F32)
    slots = []
    for start in range(0, records, LANES):
        piece = chosen[:, start:start + LANES]
        rank = jnp.dot(piece.astype(BF16), earlier, preferred_element_type=F32) + carried
        slots.append(jnp.sum(piece * rank, axis=0, keepdims=True))
        carried = carried + jnp.sum(piece, axis=1, keepdims=True)
    slot = jnp.concatenate(slots, axis=1)
    places = (iota((CAP, records), 0).astype(F32) == slot).astype(F32).astype(BF16)

    row = (cells >> 7).astype(F32)
    column = (cells & (LANES - 1)).astype(F32)
    lines = [p[n:n + 1] for p in thirds(payload) for n in range(count)] + [row, column]
    spread = jnp.concatenate([(chosen * line).astype(BF16) for line in lines], axis=0)
    packed = lax.dot_general(spread, places, (((1,), (1,)), ((), ())), preferred_element_type=F32)

    def part(index):
        return packed[index * tiles:(index + 1) * tiles]

    values = [part(n) + (part(count + n) + part(2 * count + n)) for n in range(count)]
    place = part(3 * count) * LANES + part(3 * count + 1)
    for r in range(count // 2):
        send_ref[:, r, :] = jnp.concatenate(values[2 * r:2 * r + 2], axis=1)
    for r in range(count // 2, send_ref.shape[1]):
        send_ref[:, r, :] = jnp.concatenate([place, place], axis=1)


def gathered(received, count, lon_cells):
    first = iota((received.shape[1], LANES), 1) < CAP
    spread, spots = [], []
    for s in range(0, received.shape[0], 2):
        even, odd = received[s], received[s + 1]
        low = jnp.where(first, even, pltpu.roll(odd, CAP, 1))
        high = jnp.where(first, pltpu.roll(even, CAP, 1), odd)
        cell = low[count // 2:count // 2 + 1].astype(I32)
        hit = iota((lon_cells, LANES), 0) == cell >> 7
        low, high = thirds(low), thirds(high)
        lines = [(high if n % 2 else low)[p][n // 2:n // 2 + 1]
                 for p in range(3) for n in range(count)]
        spread.append(jnp.concatenate(
            [jnp.where(hit, line, 0.0).astype(BF16) for line in lines], axis=0))
        spots.append((iota((LANES, LANES), 0) == (cell & (LANES - 1))).astype(F32).astype(BF16))
    surface = jnp.zeros((3 * count * lon_cells, LANES), F32)
    for a, b in zip(spread, spots):
        surface = surface + lax.dot_general(
            a, b, (((1,), (1,)), ((), ())), preferred_element_type=F32)
    fluxes = []
    for n in range(count):
        block = [surface[(p * count + n) * lon_cells:(p * count + n + 1) * lon_cells]
                 for p in range(3)]
        fluxes.append(block[0] + (block[1] + block[2]))
    return fluxes


def weights(speed, near, far, open_face):
    half = 0.5 * (near + far)
    return (jnp.where(open_face, jnp.maximum(speed, 0.0) + half, 0.0),
            jnp.where(open_face, jnp.minimum(speed, 0.0) - half, 0.0))


def step(tiles, *refs):
    sources, (wide, kappa_wide, east_wide, depth_wide), refs = refs[:12], refs[12:16], refs[16:]
    values, gains, refs = refs[0], refs[1], refs[2:]
    held, refs = refs[:12], refs[12:]
    (factor, share, top, fold_out, fold_in, right_in, left_in, right_depth, left_depth,
     own, halo, shifts, shifted, shifted_more, send, received, load_sems, out_sems, in_sems, pair_out, pair_in, own_sem,
     edge_sems, near, present) = refs
    (tracer, east, north, kappa, mixing, thickness, depth_ref, air, tile, source, cells,
     weight) = held
    count, planes = values.shape[:2]
    lon_cells = depth_ref.shape[0]
    levels = planes // lon_cells
    last = lon_cells - 1
    spare = LANES - levels

    pieces = [(begin, min(begin + PIECE, levels)) for begin in range(0, levels, PIECE)]
    loads = {}

    def load(i, a, b):
        loads[i] = pltpu.make_async_copy(a, b, load_sems.at[len(loads)])
        loads[i].start()

    for i in (7, 8, 9, 10, 11):
        load(i, sources[i], held[i])

    me = lax.axis_index("lon")
    right = lax.rem(me + 1, tiles)
    left = lax.rem(me + tiles - 1, tiles)
    partner = tiles - 1 - me
    barrier = pltpu.get_barrier_semaphore()

    def signal(semaphore, device):
        pl.semaphore_signal(semaphore, inc=1, device_id={"lon": device},
                            device_id_type=pl.DeviceIdType.MESH)

    @pl.loop(me + 1, tiles)
    def _(other):
        signal(barrier, other)

    load(6, sources[6], held[6])
    for p, (begin, end) in enumerate(pieces):
        block = pl.ds(begin * lon_cells, (end - begin) * lon_cells)
        moved = pl.ds(PAD + begin * lon_cells, (end - begin) * lon_cells)
        load((0, p), sources[0].at[:, block], tracer.at[:, moved])
        load((3, p), sources[3].at[block], kappa.at[moved])
        load((2, p), sources[2].at[block], north.at[block])
    for i in (5, 4, 1):
        load(i, sources[i], held[i])

    copies = []

    def copy(a, b, device):
        index = len(copies)
        copies.append(pltpu.make_async_remote_copy(
            src_ref=a, dst_ref=b, send_sem=out_sems.at[index], recv_sem=in_sems.at[index],
            device_id={"lon": device}, device_id_type=pl.DeviceIdType.MESH))
        return copies[-1]

    rows = pl.ds(0, levels)
    to_right = [
        copy(wide.at[:, :, last, 0, :], right_in.at[pl.ds(0, count), rows, :], right),
        copy(kappa_wide.at[:, last, 0, :], right_in.at[count, rows, :], right),
        copy(east_wide.at[:, last, 0, :], right_in.at[count + 1, rows, :], right),
        copy(depth_wide.at[last], right_depth, right)]
    to_left = [
        copy(wide.at[:, :, 0, 0, :], left_in.at[pl.ds(0, count), rows, :], left),
        copy(kappa_wide.at[:, 0, 0, :], left_in.at[count, rows, :], left),
        copy(depth_wide.at[0], left_depth, left)]
    to_partner = copy(fold_out, fold_in, partner)
    edges = []
    for e, i in enumerate((0, last)):
        for a, b in ((wide.at[:, :, i, 0, :], own.at[e, pl.ds(0, count), rows, :]),
                     (kappa_wide.at[:, i, 0, :], own.at[e, count, rows, :]),
                     (east_wide.at[:, i, 0, :], own.at[e, count + 1, rows, :])):
            edges.append(pltpu.make_async_copy(a, b, edge_sems.at[len(edges)]))

    def start(group):
        for each in group:
            each.start()

    def pair(other, sender):
        return pltpu.make_async_remote_copy(
            src_ref=send.at[other], dst_ref=received.at[sender], send_sem=pair_out.at[other],
            recv_sem=pair_in.at[sender], device_id={"lon": other},
            device_id_type=pl.DeviceIdType.MESH)

    @pl.when(me > 0)
    def _():
        pl.semaphore_wait(barrier, me)
        signal(near.at[0], left)
        start(to_left)

    @pl.when(me == tiles - 1)
    def _():
        signal(near.at[1], right)
        start(to_right)

    @pl.when(partner < me)
    def _():
        signal(near.at[2], partner)

    @pl.loop(0, me)
    def _(other):
        signal(present.at[me], other)

    for i in (7, 8, 9, 10, 11):
        loads[i].wait()
    route(tiles, tile[...], source[...], cells[...], weight[...], air[...], send)

    @pl.loop(0, me)
    def _(other):
        pair(other, me).start()

    mine = pltpu.make_async_copy(send.at[me], received.at[me], own_sem)
    mine.start()
    for each in edges:
        each.start()

    loads[6].wait()
    depth = depth_ref[...]

    def at(k):
        return pl.ds(pl.multiple_of(k * lon_cells, lon_cells), lon_cells)

    def beside(k, shift=0):
        start = pl.multiple_of(k * lon_cells, lon_cells) + PAD
        return pl.ds(start + shift if shift else start, lon_cells)

    lane = iota((lon_cells, LANES), 1)

    def take(k, packed):
        fields = [tracer[n, beside(k), :] for n in range(count)] + [
            kappa[beside(k), :], north[at(k), :]]
        return tuple(jnp.where(lane == k, pltpu.roll(x, k + 1, 1), p)
                     for x, p in zip(fields, packed))

    empty = jnp.zeros((lon_cells, LANES), F32)
    packed = (empty,) * (count + 2)
    for p, (begin, end) in enumerate(pieces):
        for i in (0, 3, 2):
            loads[(i, p)].wait()
        packed = lax.fori_loop(begin, end, take, packed, unroll=15)
    edge = jnp.broadcast_to(depth[:, LANES - 1:].astype(F32), (lon_cells, LANES))
    for f, plane in enumerate(packed + (edge,)):
        top[f] = plane
    sent = list(packed[:count])
    for f in range(2):
        field = packed[count + f]
        sent[2 * f] = jnp.where(lane < levels, sent[2 * f], pltpu.roll(field, levels, 1))
        sent[2 * f + 1] = jnp.where(
            lane < levels, sent[2 * f + 1], pltpu.roll(field, levels - spare, 1))
    sent[1] = jnp.where(lane == LANES - 1, edge, sent[1])
    for f, plane in enumerate(sent):
        for i in range(lon_cells):
            fold_out[f, last - i:last - i + 1, :] = plane[i:i + 1]

    @pl.when(partner < me)
    def _():
        to_partner.start()

    @pl.when(me < tiles - 1)
    def _():
        pl.semaphore_wait(near.at[0], 1)
        start(to_right)

    @pl.when(me == 0)
    def _():
        pl.semaphore_wait(near.at[1], 1)
        start(to_left)

    @pl.when(partner > me)
    def _():
        pl.semaphore_wait(near.at[2], 1)
        to_partner.start()

    @pl.loop(me + 1, tiles)
    def _(other):
        pl.semaphore_wait(present.at[other], 1)
        pair(other, me).start()

    row = iota((lon_cells, LANES), 0)
    open_east = jnp.where(row == last, 0, jnp.minimum(depth, pltpu.roll(depth, last, 0)))
    open_north = jnp.where(
        lane == LANES - 1, 0, jnp.minimum(depth, pltpu.roll(depth, LANES - 1, 1)))
    source = iota((2 * LANES, 2 * LANES), 0) & (LANES - 1)
    target = iota((2 * LANES, 2 * LANES), 1)
    target = jnp.where(target < LANES, target + 1, target - 1) & (LANES - 1)
    shifts[...] = (source == target).astype(F32).astype(BF16)
    nothing = jnp.zeros((PAD, LANES), F32)
    for side in (0, PAD + planes):
        kappa[side:side + PAD, :] = nothing
        for n in range(count):
            tracer[n, side:side + PAD, :] = nothing
    for i in (5, 4, 1):
        loads[i].wait()

    middle = (levels + 1) // 2
    chunks = levels // GROUP
    rounds = (middle + chunks // 2 - 1) // (chunks // 2)
    open_south = jnp.where(lane == 0, 0, pltpu.roll(open_north, 1, 1))

    def eliminate(k, target, coupling, prior, rest):
        here = thickness[at(k), :]
        partial = here + rest
        scale = 1.0 / (partial + coupling)
        gain = coupling * scale
        gains[at(target), :] = gain
        factor[at(target), :] = prior * scale
        share[at(target), :] = here * scale
        return gain * partial

    def below(k):
        near_by = 0.5 * (thickness[at(k), :] + thickness[at(k + 1), :])
        return jnp.where(depth > k + 1, mixing[at(k), :] / near_by, 0.0)

    def shift(c):
        lines = []
        for k in [c * GROUP + g for g in range(GROUP)]:
            for x in [tracer[n, beside(k), :] for n in range(count)] + [
                    kappa[beside(k), :], north[at(k), :]]:
                lines.append(jnp.concatenate(halves(x), axis=1))
        return jnp.dot(jnp.concatenate(lines, axis=0), shifts[...], preferred_element_type=F32)

    def face(speed, near_kappa, far_kappa, is_open):
        ahead = jnp.maximum(speed, 0.0) + 0.5 * (near_kappa + far_kappa)
        return jnp.where(is_open, ahead, 0.0), jnp.where(is_open, speed - ahead, 0.0)

    def stencil(k, g, shifted):
        def moved(f, way):
            return shifted[(g * (count + 2) + f) * lon_cells:(g * (count + 2) + f + 1) * lon_cells,
                           way * LANES:(way + 1) * LANES]

        spread = kappa[beside(k), :]
        ea, eb = face(east[at(k), :], spread, kappa[beside(k, 1), :], open_east > k)
        na, nb = face(north[at(k), :], spread, moved(count, 0), open_north > k)
        sa, sb = face(moved(count + 1, 1), moved(count, 1), spread, open_south > k)
        west = pltpu.roll(ea, 1, 0)
        centre = 1.0 - ((ea - pltpu.roll(eb, 1, 0)) + (na - sb))
        for n in range(count):
            values[n, at(k), :] = (
                (centre * tracer[n, beside(k), :] + (sa * moved(n, 1) - nb * moved(n, 0)))
                + (west * tracer[n, beside(k, -1), :] - eb * tracer[n, beside(k, 1), :]))

    def group(c, now, later):
        for g in range(GROUP):
            stencil(c * GROUP + g, g, now)
        if later is not None:
            later[...] = shift(c + 1)

    def inner(c, state):
        over, over_rest, under, under_rest = state
        for r in range(rounds):
            k = c * rounds + r
            coupling = below(k)
            over_rest = eliminate(
                k, jnp.where(k < middle, k, levels), coupling, over, over_rest)
            over = coupling
            k = levels - 1 - k
            coupling = below(k - 1)
            under_rest = eliminate(
                k, jnp.where(k >= middle, k, levels), coupling, under, under_rest)
            under = coupling
        group(2 * c, shifted, shifted_more)
        group(2 * c + 1, shifted_more, shifted)
        return over, over_rest, under, under_rest

    shifted[...] = shift(0)
    lax.fori_loop(0, chunks // 2, inner, (empty,) * 4)
    group(chunks - 1, shifted, None)

    mine.wait()

    @pl.loop(1, tiles)
    def _(hop):
        other = lax.rem(me + hop, tiles)
        pair(other, other).wait_recv()

    surface = gathered(received, count, lon_cells)
    thin = 1.0 / thickness[at(0), :]
    for n in range(count):
        values[n, at(0), :] = values[n, at(0), :] + jnp.where(depth > 0, surface[n] * thin, 0.0)

    for each in edges:
        each.wait()
    for each in copies:
        each.wait_recv()
    deep = iota((levels, LANES), 0)
    wa, wb = weights(right_in[count + 1, rows, :], right_in[count, rows, :], own[0, count, rows, :],
                     deep < jnp.minimum(right_depth[...], depth[:1]))
    ea, eb = weights(own[1, count + 1, rows, :], own[1, count, rows, :], left_in[count, rows, :],
                     deep < jnp.minimum(left_depth[...], depth[last:]))
    for n in range(count):
        halo[0, n, rows, :] = wa * right_in[n, rows, :] + wb * own[0, n, rows, :]
        halo[1, n, rows, :] = ea * own[1, n, rows, :] + eb * left_in[n, rows, :]
    came = [fold_in[n] for n in range(count)]
    kappa_far, north_far = [
        jnp.where(lane < spare, pltpu.roll(came[2 * f], spare, 1),
                  pltpu.roll(came[2 * f + 1], LANES - levels + spare, 1)) for f in range(2)]
    edge_far = jnp.broadcast_to(came[1][:, LANES - 1:], (lon_cells, LANES))
    fa, fb = weights(0.5 * (top[count + 1] - north_far), top[count], kappa_far,
                     lane < jnp.minimum(top[count + 2], edge_far).astype(I32))
    fold = [fa * top[n] + fb * came[n] for n in range(count)]

    def sweep(k, value):
        part = share[at(k), :]
        mult = factor[at(k), :]
        solved = []
        for n in range(count):
            change = jnp.where(lane == LANES - 1, pltpu.roll(fold[n], LANES - 1 - k, 1), 0.0)
            change = change - jnp.where(row == 0, halo[0, n, pl.ds(k, 1), :], 0.0)
            change = change + jnp.where(row == last, halo[1, n, pl.ds(k, 1), :], 0.0)
            solved.append(part * (values[n, at(k), :] - change) + mult * value[n])
            values[n, at(k), :] = solved[n]
        return tuple(solved)

    def both(k, state):
        return sweep(k, state[:count]) + sweep(levels - 1 - k, state[count:])

    state = lax.fori_loop(0, levels // 2, both, (empty,) * (2 * count), unroll=5)
    if levels % 2:
        sweep(levels // 2, state[:count])

    for each in copies:
        each.wait_send()

    @pl.loop(1, tiles)
    def _(hop):
        other = lax.rem(me + hop, tiles)
        pair(other, other).wait_send()


def finish(lon_cells, values, gains, out, solved, sems):
    count, planes = values.shape[:2]
    levels = planes // lon_cells
    middle = (levels + 1) // 2

    def at(k):
        return pl.ds(pl.multiple_of(k * lon_cells, lon_cells), lon_cells)

    stores = []

    def store(begin, end):
        block = pl.ds(begin * lon_cells, (end - begin) * lon_cells)
        stores.append(pltpu.make_async_copy(
            solved.at[:, block], out.at[:, block], sems.at[len(stores)]))
        stores[-1].start()

    def put(k, value):
        for n in range(count):
            solved[n, at(k), :] = value[n]

    gain, other = gains[at(middle - 1), :], gains[at(middle), :]
    over = [values[n, at(middle - 1), :] for n in range(count)]
    under = [values[n, at(middle), :] for n in range(count)]
    scale = 1.0 / (1.0 - gain * other)
    over = [(a + gain * b) * scale for a, b in zip(over, under)]
    under = [b + other * a for a, b in zip(over, under)]
    put(middle - 1, over)
    put(middle, under)

    top, bottom = middle - 1, middle + 1
    while top > 0 or bottom < levels:
        size = CHUNK - 1 if not stores else CHUNK
        for k in range(top - 1, max(top - size, 0) - 1, -1):
            gain = gains[at(k), :]
            over = [values[n, at(k), :] + gain * over[n] for n in range(count)]
            put(k, over)
        for k in range(bottom, min(bottom + size, levels)):
            gain = gains[at(k), :]
            under = [values[n, at(k), :] + gain * under[n] for n in range(count)]
            put(k, under)
        low, high = max(top - size, 0), min(bottom + size, levels)
        if not stores:
            store(low, high)
        else:
            if low < top:
                store(low, top)
            if bottom < high:
                store(bottom, high)
        top, bottom = low, high
    for each in stores:
        each.wait()


def shards(tracer, east_speed, north_speed, diffusivity, mixing, thickness, depth_levels,
           air_flux, margin_tile, margin_source, margin_cell, margin_weight):
    count, lon_cells, levels, lat_cells = tracer.shape
    tiles = lax.axis_size("lon")
    records = margin_source.shape[0]
    assert lat_cells == LANES and levels < LANES and levels // GROUP % 2 and levels % GROUP == 0

    def by_level(x):
        return x.transpose(1, 0, 2).reshape(levels * lon_cells, LANES)

    operands = (
        tracer.transpose(0, 2, 1, 3).reshape(count, levels * lon_cells, LANES),
        *[by_level(x) for x in (east_speed, north_speed, diffusivity, mixing, thickness)],
        depth_levels, air_flux,
        *[x.reshape(1, records) for x in (margin_tile, margin_source, margin_cell, margin_weight)])
    wide = (
        tracer.transpose(0, 2, 1, 3).reshape(count, levels, lon_cells, 1, LANES),
        *[x.transpose(1, 0, 2).reshape(levels, lon_cells, 1, LANES)
          for x in (diffusivity, east_speed)],
        depth_levels.reshape(lon_cells, 1, LANES))
    held = [pltpu.VMEM(x.shape, x.dtype) for x in operands]
    held[0] = pltpu.VMEM((count, levels * lon_cells + 2 * PAD, LANES), F32)
    held[3] = pltpu.VMEM((levels * lon_cells + 2 * PAD, LANES), F32)
    hbm = pl.BlockSpec(memory_space=pltpu.HBM)
    more = pltpu.VMEM(((levels + 1) * lon_cells, LANES), F32)
    rows = (levels + 7) // 8 * 8
    pairs = pltpu.VMEM((tiles, (count // 2 + 4) // 4 * 4, LANES), F32)
    moved = pltpu.VMEM((GROUP * (count + 2) * lon_cells, 2 * LANES), F32)
    dma = pltpu.SemaphoreType.DMA
    regular = pltpu.SemaphoreType.REGULAR
    vmem = pl.BlockSpec(memory_space=pltpu.VMEM)
    values, gains = pl.pallas_call(
        lambda *refs: step(tiles, *refs),
        out_shape=(pltpu.VMEM(operands[0].shape, F32), more),
        in_specs=[hbm] * 16, out_specs=(vmem, vmem),
        scratch_shapes=held + [
            more, more,
            pltpu.VMEM((count + 3, lon_cells, LANES), F32),
            pltpu.VMEM((count, lon_cells, LANES), F32), pltpu.VMEM((count, lon_cells, LANES), F32),
            pltpu.VMEM((count + 2, rows, LANES), F32), pltpu.VMEM((count + 1, rows, LANES), F32),
            pltpu.VMEM((1, LANES), I32), pltpu.VMEM((1, LANES), I32),
            pltpu.VMEM((2, count + 2, rows, LANES), F32),
            pltpu.VMEM((2, count, rows, LANES), F32),
            pltpu.VMEM((2 * LANES, 2 * LANES), BF16),
            moved, moved, pairs, pairs, dma((24,)), dma((8,)), dma((8,)),
            dma((tiles,)), dma((tiles,)), dma, dma((6,)), regular((3,)), regular((tiles,))],
        compiler_params=pltpu.CompilerParams(
            collective_id=0, has_side_effects=True, vmem_limit_bytes=32 << 20),
        name="ocean_step",
    )(*[pltpu.with_memory_space_constraint(x, pltpu.HBM) for x in operands + wide])
    result = pl.pallas_call(
        lambda *refs: finish(lon_cells, *refs),
        out_shape=pltpu.HBM(values.shape, F32),
        in_specs=[vmem, vmem], out_specs=hbm,
        scratch_shapes=[pltpu.VMEM(values.shape, F32), dma((2 * pl.cdiv(levels, 2 * CHUNK),))],
        name="finish",
    )(*[pltpu.with_memory_space_constraint(x, pltpu.VMEM) for x in (values, gains)])
    return result.reshape(count, levels, lon_cells, LANES).transpose(0, 2, 1, 3)


def solution(mesh):
    placed = (
        P(None, "lon", None, "ens"),
        P("lon", None, "ens"),
        P("lon", None, "ens"),
        P("lon", None, "ens"),
        P("lon", None, "ens"),
        P("lon", None, "ens"),
        P("lon", "ens"),
        P("ens", "lon"),
        P(("ens", "lon"), None),
        P(("ens", "lon")),
        P(("ens", "lon")),
        P(("ens", "lon")),
    )
    return jax.shard_map(
        shards, mesh=mesh, in_specs=placed, out_specs=P(None, "lon", None, "ens"), check_vma=False
    )
```

```python
import jax
import jax.numpy as jnp
from jax import lax
from jax.experimental import pallas as pl
from jax.experimental.pallas import tpu as pltpu
from jax.sharding import PartitionSpec as P

CAP = 64
CHUNK = 8
PIECE = 30
PAD = 8
GROUP = 5
EARLY = 2
LANES = 128
F32 = jnp.float32
BF16 = jnp.bfloat16
I32 = jnp.int32


def iota(shape, axis):
    return lax.broadcasted_iota(I32, shape, axis)


def thirds(x):
    high = x.astype(BF16).astype(F32)
    rest = x - high
    middle = rest.astype(BF16).astype(F32)
    return high, middle, rest - middle


def halves(x):
    high = x.astype(BF16)
    return high, (x - high.astype(F32)).astype(BF16)


def route(tiles, tile, source, cells, weight, air, send_ref):
    count, air_cells = air.shape
    records = tile.shape[1]
    picks = (iota((air_cells, records), 0) == source).astype(F32).astype(BF16)
    parts = jnp.concatenate(thirds(air), axis=0).astype(BF16)
    found = jnp.dot(parts, picks, preferred_element_type=F32)
    found = found[:count] + (found[count:2 * count] + found[2 * count:])
    payload = weight * found

    chosen = (iota((tiles, records), 0) == tile).astype(F32)
    earlier = (iota((LANES, LANES), 0) < iota((LANES, LANES), 1)).astype(F32).astype(BF16)
    carried = jnp.zeros((tiles, 1), F32)
    slots = []
    for start in range(0, records, LANES):
        piece = chosen[:, start:start + LANES]
        rank = jnp.dot(piece.astype(BF16), earlier, preferred_element_type=F32) + carried
        slots.append(jnp.sum(piece * rank, axis=0, keepdims=True))
        carried = carried + jnp.sum(piece, axis=1, keepdims=True)
    slot = jnp.concatenate(slots, axis=1)
    places = (iota((CAP, records), 0).astype(F32) == slot).astype(F32).astype(BF16)

    row = (cells >> 7).astype(F32)
    column = (cells & (LANES - 1)).astype(F32)
    lines = [p[n:n + 1] for p in thirds(payload) for n in range(count)] + [row, column]
    spread = jnp.concatenate([(chosen * line).astype(BF16) for line in lines], axis=0)
    packed = lax.dot_general(spread, places, (((1,), (1,)), ((), ())), preferred_element_type=F32)

    def part(index):
        return packed[index * tiles:(index + 1) * tiles]

    values = [part(n) + (part(count + n) + part(2 * count + n)) for n in range(count)]
    place = part(3 * count) * LANES + part(3 * count + 1)
    for r in range(count // 2):
        send_ref[:, r, :] = jnp.concatenate(values[2 * r:2 * r + 2], axis=1)
    for r in range(count // 2, send_ref.shape[1]):
        send_ref[:, r, :] = jnp.concatenate([place, place], axis=1)


def gathered(received, count, lon_cells):
    first = iota((received.shape[1], LANES), 1) < CAP
    spread, spots = [], []
    for s in range(0, received.shape[0], 2):
        even, odd = received[s], received[s + 1]
        low = jnp.where(first, even, pltpu.roll(odd, CAP, 1))
        high = jnp.where(first, pltpu.roll(even, CAP, 1), odd)
        cell = low[count // 2:count // 2 + 1].astype(I32)
        hit = iota((lon_cells, LANES), 0) == cell >> 7
        low, high = thirds(low), thirds(high)
        lines = [(high if n % 2 else low)[p][n // 2:n // 2 + 1]
                 for p in range(3) for n in range(count)]
        spread.append(jnp.concatenate(
            [jnp.where(hit, line, 0.0).astype(BF16) for line in lines], axis=0))
        spots.append((iota((LANES, LANES), 0) == (cell & (LANES - 1))).astype(F32).astype(BF16))
    surface = jnp.zeros((3 * count * lon_cells, LANES), F32)
    for a, b in zip(spread, spots):
        surface = surface + lax.dot_general(
            a, b, (((1,), (1,)), ((), ())), preferred_element_type=F32)
    fluxes = []
    for n in range(count):
        block = [surface[(p * count + n) * lon_cells:(p * count + n + 1) * lon_cells]
                 for p in range(3)]
        fluxes.append(block[0] + (block[1] + block[2]))
    return fluxes


def weights(speed, near, far, open_face):
    half = 0.5 * (near + far)
    return (jnp.where(open_face, jnp.maximum(speed, 0.0) + half, 0.0),
            jnp.where(open_face, jnp.minimum(speed, 0.0) - half, 0.0))


def step(tiles, *refs):
    sources, (wide, kappa_wide, east_wide, depth_wide), refs = refs[:12], refs[12:16], refs[16:]
    values, gains, refs = refs[0], refs[1], refs[2:]
    held, refs = refs[:12], refs[12:]
    (factor, share, top, fold_out, fold_in, right_in, left_in, right_depth, left_depth,
     own, halo, shifts, shifted, shifted_more, send, received, load_sems, out_sems, in_sems, pair_out, pair_in, own_sem,
     edge_sems, near, present) = refs
    (tracer, east, north, kappa, mixing, thickness, depth_ref, air, tile, source, cells,
     weight) = held
    count, planes = values.shape[:2]
    lon_cells = depth_ref.shape[0]
    levels = planes // lon_cells
    last = lon_cells - 1
    spare = LANES - levels

    pieces = [(begin, min(begin + PIECE, levels)) for begin in range(0, levels, PIECE)]
    loads = {}

    def load(i, a, b):
        loads[i] = pltpu.make_async_copy(a, b, load_sems.at[len(loads)])
        loads[i].start()

    for i in (7, 8, 9, 10, 11):
        load(i, sources[i], held[i])

    me = lax.axis_index("lon")
    right = lax.rem(me + 1, tiles)
    left = lax.rem(me + tiles - 1, tiles)
    partner = tiles - 1 - me
    barrier = pltpu.get_barrier_semaphore()

    def signal(semaphore, device):
        pl.semaphore_signal(semaphore, inc=1, device_id={"lon": device},
                            device_id_type=pl.DeviceIdType.MESH)

    load(6, sources[6], held[6])
    for p, (begin, end) in enumerate(pieces):
        block = pl.ds(begin * lon_cells, (end - begin) * lon_cells)
        moved = pl.ds(PAD + begin * lon_cells, (end - begin) * lon_cells)
        load((0, p), sources[0].at[:, block], tracer.at[:, moved])
        load((3, p), sources[3].at[block], kappa.at[moved])
        load((2, p), sources[2].at[block], north.at[block])
    for i in (5, 4, 1):
        load(i, sources[i], held[i])

    @pl.loop(me + 1, tiles)
    def _(other):
        signal(barrier, other)

    copies = []

    def copy(a, b, device):
        index = len(copies)
        copies.append(pltpu.make_async_remote_copy(
            src_ref=a, dst_ref=b, send_sem=out_sems.at[index], recv_sem=in_sems.at[index],
            device_id={"lon": device}, device_id_type=pl.DeviceIdType.MESH))
        return copies[-1]

    rows = pl.ds(0, levels)
    def halo_copies(i, into, into_depth, singles, device):
        some, more = pl.ds(0, count // 2), pl.ds(count // 2, count - count // 2)
        rest = [(wide.at[more, :, i, 0, :], into.at[more, rows, :])]
        rest += [(x.at[:, i, 0, :], into.at[count + f, rows, :]) for f, x in enumerate(singles)]
        rest += [(depth_wide.at[i], into_depth)]
        return ([copy(wide.at[some, :, i, 0, :], into.at[some, rows, :], device)],
                [copy(x, y, device) for x, y in rest])

    to_right = halo_copies(last, right_in, right_depth, (kappa_wide, east_wide), right)
    to_left = halo_copies(0, left_in, left_depth, (kappa_wide,), left)
    to_partner = copy(fold_out, fold_in, partner)
    edges = []
    for e, i in enumerate((0, last)):
        for a, b in ((wide.at[:, :, i, 0, :], own.at[e, pl.ds(0, count), rows, :]),
                     (kappa_wide.at[:, i, 0, :], own.at[e, count, rows, :]),
                     (east_wide.at[:, i, 0, :], own.at[e, count + 1, rows, :])):
            edges.append(pltpu.make_async_copy(a, b, edge_sems.at[len(edges)]))

    def start(group):
        for each in group:
            each.start()

    def pair(other, sender):
        return pltpu.make_async_remote_copy(
            src_ref=send.at[other], dst_ref=received.at[sender], send_sem=pair_out.at[other],
            recv_sem=pair_in.at[sender], device_id={"lon": other},
            device_id_type=pl.DeviceIdType.MESH)

    even = lax.rem(me, 2) == 0
    topmost = me == tiles - 1
    early = jnp.logical_and(me < EARLY, lax.axis_index("ens") == 0)

    def when(*conditions):
        met = conditions[0]
        for each in conditions[1:]:
            met = jnp.logical_and(met, each)
        return pl.when(met)

    @pl.when(me > 0)
    def _():
        pl.semaphore_wait(barrier, me)
        signal(near.at[0], left)

    @when(even, me > 0)
    def _():
        start(to_left[0])

    @when(jnp.logical_not(even), me < tiles - 1)
    def _():
        start(to_left[0] + to_left[1])

    @when(topmost)
    def _():
        start(to_right[0])

    @pl.when(me == tiles - 1)
    def _():
        signal(near.at[1], right)

    @pl.when(partner < me)
    def _():
        signal(near.at[2], partner)

    @pl.loop(0, me)
    def _(other):
        signal(present.at[me], other)

    for i in (7, 8, 9, 10, 11):
        loads[i].wait()
    route(tiles, tile[...], source[...], cells[...], weight[...], air[...], send)

    @pl.loop(0, me)
    def _(other):
        pair(other, me).start()

    @pl.when(me < tiles - 1)
    def _():
        pl.semaphore_wait(near.at[0], 1)
        start(to_right[0])

    @when(jnp.logical_or(jnp.logical_or(even, me < tiles // 2), topmost))
    def _():
        start(to_right[1])

    @when(even, me > 0, me < tiles // 2)
    def _():
        start(to_left[1])

    mine = pltpu.make_async_copy(send.at[me], received.at[me], own_sem)
    mine.start()
    for each in edges:
        each.start()

    loads[6].wait()
    depth = depth_ref[...]

    def at(k):
        return pl.ds(pl.multiple_of(k * lon_cells, lon_cells), lon_cells)

    def beside(k, shift=0):
        start = pl.multiple_of(k * lon_cells, lon_cells) + PAD
        return pl.ds(start + shift if shift else start, lon_cells)

    lane = iota((lon_cells, LANES), 1)

    def split(k):
        return [jnp.concatenate(halves(x), axis=1) for x in
                [tracer[n, beside(k), :] for n in range(count)] + [
                    kappa[beside(k), :], north[at(k), :]]]

    def take(k, packed):
        fields = [tracer[n, beside(k), :] for n in range(count)] + [
            kappa[beside(k), :], north[at(k), :]]
        return tuple(jnp.where(lane == k, pltpu.roll(x, k + 1, 1), p)
                     for x, p in zip(fields, packed))

    empty = jnp.zeros((lon_cells, LANES), F32)
    packed = (empty,) * (count + 2)
    for p, (begin, end) in enumerate(pieces):
        for i in (0, 3, 2):
            loads[(i, p)].wait()
        packed = lax.fori_loop(begin, end, take, packed, unroll=15)
    edge = jnp.broadcast_to(depth[:, LANES - 1:].astype(F32), (lon_cells, LANES))
    for f, plane in enumerate(packed + (edge,)):
        top[f] = plane
    sent = list(packed[:count])
    for f in range(2):
        field = packed[count + f]
        sent[2 * f] = jnp.where(lane < levels, sent[2 * f], pltpu.roll(field, levels, 1))
        sent[2 * f + 1] = jnp.where(
            lane < levels, sent[2 * f + 1], pltpu.roll(field, levels - spare, 1))
    sent[1] = jnp.where(lane == LANES - 1, edge, sent[1])
    for f, plane in enumerate(sent):
        for i in range(lon_cells):
            fold_out[f, last - i:last - i + 1, :] = plane[i:i + 1]

    @pl.when(partner < me)
    def _():
        to_partner.start()

    def answer():
        @pl.loop(me + 1, tiles)
        def _(other):
            pl.semaphore_wait(present.at[other], 1)
            pair(other, me).start()

        @pl.when(partner > me)
        def _():
            pl.semaphore_wait(near.at[2], 1)
            to_partner.start()

        @pl.when(me == 0)
        def _():
            pl.semaphore_wait(near.at[1], 1)
            start(to_left[0] + to_left[1])

    @when(even, me >= tiles // 2)
    def _():
        start(to_left[1])

    @when(jnp.logical_not(early))
    def _():
        answer()

    @when(jnp.logical_not(even), me >= tiles // 2, me < tiles - 1)
    def _():
        start(to_right[1])

    @when(topmost)
    def _():
        start(to_left[0] + to_left[1])

    row = iota((lon_cells, LANES), 0)
    open_east = jnp.where(row == last, 0, jnp.minimum(depth, pltpu.roll(depth, last, 0)))
    open_north = jnp.where(
        lane == LANES - 1, 0, jnp.minimum(depth, pltpu.roll(depth, LANES - 1, 1)))
    source = iota((2 * LANES, 2 * LANES), 0) & (LANES - 1)
    target = iota((2 * LANES, 2 * LANES), 1)
    target = jnp.where(target < LANES, target + 1, target - 1) & (LANES - 1)
    shifts[...] = (source == target).astype(F32).astype(BF16)
    nothing = jnp.zeros((PAD, LANES), F32)
    for side in (0, PAD + planes):
        kappa[side:side + PAD, :] = nothing
        for n in range(count):
            tracer[n, side:side + PAD, :] = nothing
    for i in (5, 4, 1):
        loads[i].wait()

    middle = (levels + 1) // 2
    chunks = levels // GROUP
    rounds = (middle + chunks // 2 - 1) // (chunks // 2)
    open_south = jnp.where(lane == 0, 0, pltpu.roll(open_north, 1, 1))

    def eliminate(k, target, coupling, prior, rest):
        here = thickness[at(k), :]
        partial = here + rest
        scale = 1.0 / (partial + coupling)
        gain = coupling * scale
        gains[at(target), :] = gain
        factor[at(target), :] = prior * scale
        share[at(target), :] = here * scale
        return gain * partial

    def below(k):
        near_by = 0.5 * (thickness[at(k), :] + thickness[at(k + 1), :])
        return jnp.where(depth > k + 1, mixing[at(k), :] / near_by, 0.0)

    def shift(c):
        lines = jnp.concatenate(
            [x for g in range(GROUP) for x in split(c * GROUP + g)], axis=0)
        return jnp.dot(lines, shifts[...], preferred_element_type=F32)

    def face(speed, near_kappa, far_kappa, is_open):
        ahead = jnp.maximum(speed, 0.0) + 0.5 * (near_kappa + far_kappa)
        return jnp.where(is_open, ahead, 0.0), jnp.where(is_open, speed - ahead, 0.0)

    def stencil(k, g, shifted):
        def moved(f, way):
            return shifted[(g * (count + 2) + f) * lon_cells:(g * (count + 2) + f + 1) * lon_cells,
                           way * LANES:(way + 1) * LANES]

        spread = kappa[beside(k), :]
        ea, eb = face(east[at(k), :], spread, kappa[beside(k, 1), :], open_east > k)
        na, nb = face(north[at(k), :], spread, moved(count, 0), open_north > k)
        sa, sb = face(moved(count + 1, 1), moved(count, 1), spread, open_south > k)
        west = pltpu.roll(ea, 1, 0)
        centre = 1.0 - ((ea - pltpu.roll(eb, 1, 0)) + (na - sb))
        for n in range(count):
            values[n, at(k), :] = (
                (centre * tracer[n, beside(k), :] + (sa * moved(n, 1) - nb * moved(n, 0)))
                + (west * tracer[n, beside(k, -1), :] - eb * tracer[n, beside(k, 1), :]))

    def group(c, now, later):
        for g in range(GROUP):
            stencil(c * GROUP + g, g, now)
        if later is not None:
            later[...] = shift(c + 1)

    def inner(c, state):
        over, over_rest, under, under_rest = state
        for r in range(rounds):
            k = c * rounds + r
            coupling = below(k)
            over_rest = eliminate(
                k, jnp.where(k < middle, k, levels), coupling, over, over_rest)
            over = coupling
            k = levels - 1 - k
            coupling = below(k - 1)
            under_rest = eliminate(
                k, jnp.where(k >= middle, k, levels), coupling, under, under_rest)
            under = coupling
        group(2 * c, shifted, shifted_more)
        group(2 * c + 1, shifted_more, shifted)
        return over, over_rest, under, under_rest

    shifted[...] = shift(0)
    lax.fori_loop(0, chunks // 2, inner, (empty,) * 4)
    group(chunks - 1, shifted, None)

    @when(early)
    def _():
        answer()

    mine.wait()

    @pl.loop(1, tiles)
    def _(hop):
        other = lax.rem(me + hop, tiles)
        pair(other, other).wait_recv()

    surface = gathered(received, count, lon_cells)
    thin = 1.0 / thickness[at(0), :]
    for n in range(count):
        values[n, at(0), :] = values[n, at(0), :] + jnp.where(depth > 0, surface[n] * thin, 0.0)

    for each in copies:
        each.wait_send()

    @pl.loop(1, tiles)
    def _(hop):
        other = lax.rem(me + hop, tiles)
        pair(other, other).wait_send()

    for each in edges:
        each.wait()
    for each in to_right[0] + to_right[1] + to_left[0] + to_left[1]:
        each.wait_recv()
    deep = iota((levels, LANES), 0)
    wa, wb = weights(right_in[count + 1, rows, :], right_in[count, rows, :], own[0, count, rows, :],
                     deep < jnp.minimum(right_depth[...], depth[:1]))
    ea, eb = weights(own[1, count + 1, rows, :], own[1, count, rows, :], left_in[count, rows, :],
                     deep < jnp.minimum(left_depth[...], depth[last:]))
    for n in range(count):
        halo[0, n, rows, :] = -(wa * right_in[n, rows, :] + wb * own[0, n, rows, :])
        halo[1, n, rows, :] = ea * own[1, n, rows, :] + eb * left_in[n, rows, :]
    to_partner.wait_recv()
    came = [fold_in[n] for n in range(count)]
    kappa_far, north_far = [
        jnp.where(lane < spare, pltpu.roll(came[2 * f], spare, 1),
                  pltpu.roll(came[2 * f + 1], LANES - levels + spare, 1)) for f in range(2)]
    edge_far = jnp.broadcast_to(came[1][:, LANES - 1:], (lon_cells, LANES))
    fa, fb = weights(0.5 * (top[count + 1] - north_far), top[count], kappa_far,
                     lane < jnp.minimum(top[count + 2], edge_far).astype(I32))
    fold = [fa * top[n] + fb * came[n] for n in range(count)]
    half = lon_cells // 2
    line = iota((half, LANES), 0)

    def sweep(k, value):
        part = share[at(k), :]
        mult = factor[at(k), :]
        solved = []
        for n in range(count):
            sides = jnp.concatenate(
                [jnp.where(line == 0, halo[0, n, pl.ds(k, 1), :], 0.0),
                 jnp.where(line == half - 1, halo[1, n, pl.ds(k, 1), :], 0.0)], axis=0)
            across = jnp.where(lane == LANES - 1, pltpu.roll(fold[n], LANES - 1 - k, 1), 0.0)
            solved.append(part * (values[n, at(k), :] - (across + sides)) + mult * value[n])
            values[n, at(k), :] = solved[n]
        return tuple(solved)

    def both(k, state):
        return sweep(k, state[:count]) + sweep(levels - 1 - k, state[count:])

    state = lax.fori_loop(0, levels // 2, both, (empty,) * (2 * count), unroll=5)
    if levels % 2:
        sweep(levels // 2, state[:count])


def finish(lon_cells, values, gains, out, solved, sems):
    count, planes = values.shape[:2]
    levels = planes // lon_cells
    middle = (levels + 1) // 2

    def at(k):
        return pl.ds(pl.multiple_of(k * lon_cells, lon_cells), lon_cells)

    stores = []

    def store(begin, end):
        block = pl.ds(begin * lon_cells, (end - begin) * lon_cells)
        stores.append(pltpu.make_async_copy(
            solved.at[:, block], out.at[:, block], sems.at[len(stores)]))
        stores[-1].start()

    def put(k, value):
        for n in range(count):
            solved[n, at(k), :] = value[n]

    gain, other = gains[at(middle - 1), :], gains[at(middle), :]
    over = [values[n, at(middle - 1), :] for n in range(count)]
    under = [values[n, at(middle), :] for n in range(count)]
    scale = 1.0 / (1.0 - gain * other)
    over = [(a + gain * b) * scale for a, b in zip(over, under)]
    under = [b + other * a for a, b in zip(over, under)]
    put(middle - 1, over)
    put(middle, under)

    top, bottom = middle - 1, middle + 1
    while top > 0 or bottom < levels:
        size = CHUNK - 1 if not stores else CHUNK
        for k in range(top - 1, max(top - size, 0) - 1, -1):
            gain = gains[at(k), :]
            over = [values[n, at(k), :] + gain * over[n] for n in range(count)]
            put(k, over)
        for k in range(bottom, min(bottom + size, levels)):
            gain = gains[at(k), :]
            under = [values[n, at(k), :] + gain * under[n] for n in range(count)]
            put(k, under)
        low, high = max(top - size, 0), min(bottom + size, levels)
        if not stores:
            store(low, high)
        else:
            if low < top:
                store(low, top)
            if bottom < high:
                store(bottom, high)
        top, bottom = low, high
    for each in stores:
        each.wait()


def shards(tracer, east_speed, north_speed, diffusivity, mixing, thickness, depth_levels,
           air_flux, margin_tile, margin_source, margin_cell, margin_weight):
    count, lon_cells, levels, lat_cells = tracer.shape
    tiles = lax.axis_size("lon")
    records = margin_source.shape[0]
    assert lat_cells == LANES and levels < LANES and levels // GROUP % 2 and levels % GROUP == 0

    def by_level(x):
        return x.transpose(1, 0, 2).reshape(levels * lon_cells, LANES)

    operands = (
        tracer.transpose(0, 2, 1, 3).reshape(count, levels * lon_cells, LANES),
        *[by_level(x) for x in (east_speed, north_speed, diffusivity, mixing, thickness)],
        depth_levels, air_flux,
        *[x.reshape(1, records) for x in (margin_tile, margin_source, margin_cell, margin_weight)])
    wide = (
        tracer.transpose(0, 2, 1, 3).reshape(count, levels, lon_cells, 1, LANES),
        *[x.transpose(1, 0, 2).reshape(levels, lon_cells, 1, LANES)
          for x in (diffusivity, east_speed)],
        depth_levels.reshape(lon_cells, 1, LANES))
    held = [pltpu.VMEM(x.shape, x.dtype) for x in operands]
    held[0] = pltpu.VMEM((count, levels * lon_cells + 2 * PAD, LANES), F32)
    held[3] = pltpu.VMEM((levels * lon_cells + 2 * PAD, LANES), F32)
    hbm = pl.BlockSpec(memory_space=pltpu.HBM)
    more = pltpu.VMEM(((levels + 1) * lon_cells, LANES), F32)
    rows = (levels + 7) // 8 * 8
    pairs = pltpu.VMEM((tiles, (count // 2 + 4) // 4 * 4, LANES), F32)
    moved = pltpu.VMEM((GROUP * (count + 2) * lon_cells, 2 * LANES), F32)
    dma = pltpu.SemaphoreType.DMA
    regular = pltpu.SemaphoreType.REGULAR
    vmem = pl.BlockSpec(memory_space=pltpu.VMEM)
    values, gains = pl.pallas_call(
        lambda *refs: step(tiles, *refs),
        out_shape=(pltpu.VMEM(operands[0].shape, F32), more),
        in_specs=[hbm] * 16, out_specs=(vmem, vmem),
        scratch_shapes=held + [
            more, more,
            pltpu.VMEM((count + 3, lon_cells, LANES), F32),
            pltpu.VMEM((count, lon_cells, LANES), F32), pltpu.VMEM((count, lon_cells, LANES), F32),
            pltpu.VMEM((count + 2, rows, LANES), F32), pltpu.VMEM((count + 1, rows, LANES), F32),
            pltpu.VMEM((1, LANES), I32), pltpu.VMEM((1, LANES), I32),
            pltpu.VMEM((2, count + 2, rows, LANES), F32),
            pltpu.VMEM((2, count, rows, LANES), F32),
            pltpu.VMEM((2 * LANES, 2 * LANES), BF16),
            moved, moved, pairs, pairs, dma((24,)), dma((12,)), dma((12,)),
            dma((tiles,)), dma((tiles,)), dma, dma((6,)), regular((3,)), regular((tiles,))],
        compiler_params=pltpu.CompilerParams(
            collective_id=0, has_side_effects=True, vmem_limit_bytes=32 << 20),
        name="ocean_step",
    )(*[pltpu.with_memory_space_constraint(x, pltpu.HBM) for x in operands + wide])
    result = pl.pallas_call(
        lambda *refs: finish(lon_cells, *refs),
        out_shape=pltpu.HBM(values.shape, F32),
        in_specs=[vmem, vmem], out_specs=hbm,
        scratch_shapes=[pltpu.VMEM(values.shape, F32), dma((2 * pl.cdiv(levels, 2 * CHUNK),))],
        name="finish",
    )(*[pltpu.with_memory_space_constraint(x, pltpu.VMEM) for x in (values, gains)])
    return result.reshape(count, levels, lon_cells, LANES).transpose(0, 2, 1, 3)


def solution(mesh):
    placed = (
        P(None, "lon", None, "ens"),
        P("lon", None, "ens"),
        P("lon", None, "ens"),
        P("lon", None, "ens"),
        P("lon", None, "ens"),
        P("lon", None, "ens"),
        P("lon", "ens"),
        P("ens", "lon"),
        P(("ens", "lon"), None),
        P(("ens", "lon")),
        P(("ens", "lon")),
        P(("ens", "lon")),
    )
    return jax.shard_map(
        shards, mesh=mesh, in_specs=placed, out_specs=P(None, "lon", None, "ens"), check_vma=False
    )
```

```python
import jax
import jax.numpy as jnp
from jax import lax
from jax.experimental import pallas as pl
from jax.experimental.pallas import tpu as pltpu
from jax.sharding import PartitionSpec as P

CAP = 64
CHUNK = 8
PIECE = 30
BATCH = 15
SPLIT = 2
PAD = 8
GROUP = 5
EARLY = 2
LANES = 128
F32 = jnp.float32
BF16 = jnp.bfloat16
I32 = jnp.int32


def iota(shape, axis):
    return lax.broadcasted_iota(I32, shape, axis)


def thirds(x):
    high = x.astype(BF16).astype(F32)
    rest = x - high
    middle = rest.astype(BF16).astype(F32)
    return high, middle, rest - middle


def halves(x):
    high = x.astype(BF16)
    return high, (x - high.astype(F32)).astype(BF16)


def route(tiles, tile, source, cells, weight, air, send_ref):
    count, air_cells = air.shape
    records = tile.shape[1]
    picks = (iota((air_cells, records), 0) == source).astype(F32).astype(BF16)
    parts = jnp.concatenate(thirds(air), axis=0).astype(BF16)
    found = jnp.dot(parts, picks, preferred_element_type=F32)
    found = found[:count] + (found[count:2 * count] + found[2 * count:])
    payload = weight * found

    chosen = (iota((tiles, records), 0) == tile).astype(F32)
    earlier = (iota((LANES, LANES), 0) < iota((LANES, LANES), 1)).astype(F32).astype(BF16)
    carried = jnp.zeros((tiles, 1), F32)
    slots = []
    for start in range(0, records, LANES):
        piece = chosen[:, start:start + LANES]
        rank = jnp.dot(piece.astype(BF16), earlier, preferred_element_type=F32) + carried
        slots.append(jnp.sum(piece * rank, axis=0, keepdims=True))
        carried = carried + jnp.sum(piece, axis=1, keepdims=True)
    slot = jnp.concatenate(slots, axis=1)
    places = (iota((CAP, records), 0).astype(F32) == slot).astype(F32).astype(BF16)

    row = (cells >> 7).astype(F32)
    column = (cells & (LANES - 1)).astype(F32)
    lines = [p[n:n + 1] for p in thirds(payload) for n in range(count)] + [row, column]
    spread = jnp.concatenate([(chosen * line).astype(BF16) for line in lines], axis=0)
    packed = lax.dot_general(spread, places, (((1,), (1,)), ((), ())), preferred_element_type=F32)

    def part(index):
        return packed[index * tiles:(index + 1) * tiles]

    values = [part(n) + (part(count + n) + part(2 * count + n)) for n in range(count)]
    place = part(3 * count) * LANES + part(3 * count + 1)
    for r in range(count // 2):
        send_ref[:, r, :] = jnp.concatenate(values[2 * r:2 * r + 2], axis=1)
    for r in range(count // 2, send_ref.shape[1]):
        send_ref[:, r, :] = jnp.concatenate([place, place], axis=1)


def gathered(received, count, lon_cells):
    first = iota((received.shape[1], LANES), 1) < CAP
    spread, spots = [], []
    for s in range(0, received.shape[0], 2):
        even, odd = received[s], received[s + 1]
        low = jnp.where(first, even, pltpu.roll(odd, CAP, 1))
        high = jnp.where(first, pltpu.roll(even, CAP, 1), odd)
        cell = low[count // 2:count // 2 + 1].astype(I32)
        hit = iota((lon_cells, LANES), 0) == cell >> 7
        low, high = thirds(low), thirds(high)
        lines = [(high if n % 2 else low)[p][n // 2:n // 2 + 1]
                 for p in range(3) for n in range(count)]
        spread.append(jnp.concatenate(
            [jnp.where(hit, line, 0.0).astype(BF16) for line in lines], axis=0))
        spots.append((iota((LANES, LANES), 0) == (cell & (LANES - 1))).astype(F32).astype(BF16))
    surface = jnp.zeros((3 * count * lon_cells, LANES), F32)
    for a, b in zip(spread, spots):
        surface = surface + lax.dot_general(
            a, b, (((1,), (1,)), ((), ())), preferred_element_type=F32)
    fluxes = []
    for n in range(count):
        block = [surface[(p * count + n) * lon_cells:(p * count + n + 1) * lon_cells]
                 for p in range(3)]
        fluxes.append(block[0] + (block[1] + block[2]))
    return fluxes


def weights(speed, near, far, open_face):
    half = 0.5 * (near + far)
    return (jnp.where(open_face, jnp.maximum(speed, 0.0) + half, 0.0),
            jnp.where(open_face, jnp.minimum(speed, 0.0) - half, 0.0))


def step(tiles, *refs):
    sources, (wide, kappa_wide, east_wide, depth_wide), refs = refs[:12], refs[12:16], refs[16:]
    values, gains, refs = refs[0], refs[1], refs[2:]
    held, refs = refs[:12], refs[12:]
    (factor, share, top, fold_out, fold_in, right_in, left_in, right_depth, left_depth,
     own, halo, shifts, shifted, shifted_more, send, received, load_sems, out_sems, in_sems, pair_out, pair_in, own_sem,
     edge_sems, near, present) = refs
    (tracer, east, north, kappa, mixing, thickness, depth_ref, air, tile, source, cells,
     weight) = held
    count, planes = values.shape[:2]
    lon_cells = depth_ref.shape[0]
    levels = planes // lon_cells
    last = lon_cells - 1
    spare = LANES - levels

    pieces = [(begin, min(begin + PIECE, levels)) for begin in range(0, levels, PIECE)]
    loads = {}

    def load(i, a, b):
        loads[i] = pltpu.make_async_copy(a, b, load_sems.at[len(loads)])
        loads[i].start()

    for i in (7, 8, 9, 10, 11):
        load(i, sources[i], held[i])

    me = lax.axis_index("lon")
    right = lax.rem(me + 1, tiles)
    left = lax.rem(me + tiles - 1, tiles)
    partner = tiles - 1 - me
    barrier = pltpu.get_barrier_semaphore()

    def signal(semaphore, device):
        pl.semaphore_signal(semaphore, inc=1, device_id={"lon": device},
                            device_id_type=pl.DeviceIdType.MESH)

    load(6, sources[6], held[6])
    for p, (begin, end) in enumerate(pieces):
        block = pl.ds(begin * lon_cells, (end - begin) * lon_cells)
        moved = pl.ds(PAD + begin * lon_cells, (end - begin) * lon_cells)
        load((0, p), sources[0].at[:, block], tracer.at[:, moved])
        load((3, p), sources[3].at[block], kappa.at[moved])
        load((2, p), sources[2].at[block], north.at[block])
    for i in (5, 4, 1):
        load(i, sources[i], held[i])

    @pl.loop(me + 1, tiles)
    def _(other):
        signal(barrier, other)

    copies = []

    def copy(a, b, device):
        index = len(copies)
        copies.append(pltpu.make_async_remote_copy(
            src_ref=a, dst_ref=b, send_sem=out_sems.at[index], recv_sem=in_sems.at[index],
            device_id={"lon": device}, device_id_type=pl.DeviceIdType.MESH))
        return copies[-1]

    rows = pl.ds(0, levels)
    def halo_copies(i, into, into_depth, singles, device):
        some, more = pl.ds(0, count // 2), pl.ds(count // 2, count - count // 2)
        rest = [(wide.at[more, :, i, 0, :], into.at[more, rows, :])]
        rest += [(x.at[:, i, 0, :], into.at[count + f, rows, :]) for f, x in enumerate(singles)]
        rest += [(depth_wide.at[i], into_depth)]
        return ([copy(wide.at[some, :, i, 0, :], into.at[some, rows, :], device)],
                [copy(x, y, device) for x, y in rest])

    to_right = halo_copies(last, right_in, right_depth, (kappa_wide, east_wide), right)
    to_left = halo_copies(0, left_in, left_depth, (kappa_wide,), left)
    to_partner = copy(fold_out, fold_in, partner)
    edges = []
    for e, i in enumerate((0, last)):
        for a, b in ((wide.at[:, :, i, 0, :], own.at[e, pl.ds(0, count), rows, :]),
                     (kappa_wide.at[:, i, 0, :], own.at[e, count, rows, :]),
                     (east_wide.at[:, i, 0, :], own.at[e, count + 1, rows, :])):
            edges.append(pltpu.make_async_copy(a, b, edge_sems.at[len(edges)]))

    def start(group):
        for each in group:
            each.start()

    def pair(other, sender):
        return pltpu.make_async_remote_copy(
            src_ref=send.at[other], dst_ref=received.at[sender], send_sem=pair_out.at[other],
            recv_sem=pair_in.at[sender], device_id={"lon": other},
            device_id_type=pl.DeviceIdType.MESH)

    even = lax.rem(me, 2) == 0
    topmost = me == tiles - 1
    early = jnp.logical_and(me < EARLY, lax.axis_index("ens") == 0)

    def when(*conditions):
        met = conditions[0]
        for each in conditions[1:]:
            met = jnp.logical_and(met, each)
        return pl.when(met)

    @pl.when(me > 0)
    def _():
        pl.semaphore_wait(barrier, me)
        signal(near.at[0], left)

    @when(even, me > 0)
    def _():
        start(to_left[0])

    @when(jnp.logical_not(even), me < tiles - 1)
    def _():
        start(to_left[0] + to_left[1])

    @when(topmost)
    def _():
        start(to_right[0])

    @pl.when(me == tiles - 1)
    def _():
        signal(near.at[1], right)

    @pl.when(partner < me)
    def _():
        signal(near.at[2], partner)

    @pl.loop(0, me)
    def _(other):
        signal(present.at[me], other)

    for i in (7, 8, 9, 10, 11):
        loads[i].wait()
    route(tiles, tile[...], source[...], cells[...], weight[...], air[...], send)

    @pl.loop(0, me)
    def _(other):
        pair(other, me).start()

    @pl.when(me < tiles - 1)
    def _():
        pl.semaphore_wait(near.at[0], 1)
        start(to_right[0])

    @when(jnp.logical_or(jnp.logical_or(even, me < tiles // 2), topmost))
    def _():
        start(to_right[1])

    @when(even, me > 0, me < tiles // 2)
    def _():
        start(to_left[1])

    mine = pltpu.make_async_copy(send.at[me], received.at[me], own_sem)
    mine.start()
    for each in edges:
        each.start()

    loads[6].wait()
    depth = depth_ref[...]

    def at(k):
        return pl.ds(pl.multiple_of(k * lon_cells, lon_cells), lon_cells)

    def beside(k, shift=0):
        start = pl.multiple_of(k * lon_cells, lon_cells) + PAD
        return pl.ds(start + shift if shift else start, lon_cells)

    lane = iota((lon_cells, LANES), 1)

    def split(k):
        return [jnp.concatenate(halves(x), axis=1) for x in
                [tracer[n, beside(k), :] for n in range(count)] + [
                    kappa[beside(k), :], north[at(k), :]]]

    far_lane = iota((2 * LANES, LANES), 0) & (LANES - 1)
    spread_last = (far_lane == LANES - 1).astype(F32).astype(BF16)

    def take(c, packed):
        ks = [c * BATCH + g for g in range(BATCH)]
        lines = [jnp.concatenate(halves(tracer[n, beside(k), :]), axis=1)
                 for k in ks for n in range(SPLIT)]
        found = jnp.dot(
            jnp.concatenate(lines, axis=0), spread_last, preferred_element_type=F32)
        packed = list(packed)
        for g, k in enumerate(ks):
            fields = [found[(g * SPLIT + n) * lon_cells:(g * SPLIT + n + 1) * lon_cells]
                      for n in range(SPLIT)]
            fields += [pltpu.roll(x, k + 1, 1) for x in
                       [tracer[n, beside(k), :] for n in range(SPLIT, count)] + [
                           kappa[beside(k), :], north[at(k), :]]]
            packed = [jnp.where(lane == k, x, p) for x, p in zip(fields, packed)]
        return tuple(packed)

    empty = jnp.zeros((lon_cells, LANES), F32)
    packed = (empty,) * (count + 2)
    for p, (begin, end) in enumerate(pieces):
        for i in (0, 3, 2):
            loads[(i, p)].wait()
        packed = lax.fori_loop(begin // BATCH, end // BATCH, take, packed)
    edge = jnp.broadcast_to(depth[:, LANES - 1:].astype(F32), (lon_cells, LANES))
    for f, plane in enumerate(packed + (edge,)):
        top[f] = plane
    sent = list(packed[:count])
    for f in range(2):
        field = packed[count + f]
        sent[2 * f] = jnp.where(lane < levels, sent[2 * f], pltpu.roll(field, levels, 1))
        sent[2 * f + 1] = jnp.where(
            lane < levels, sent[2 * f + 1], pltpu.roll(field, levels - spare, 1))
    sent[1] = jnp.where(lane == LANES - 1, edge, sent[1])
    for f, plane in enumerate(sent):
        for i in range(lon_cells):
            fold_out[f, last - i:last - i + 1, :] = plane[i:i + 1]

    @pl.when(partner < me)
    def _():
        to_partner.start()

    def answer():
        @pl.loop(me + 1, tiles)
        def _(other):
            pl.semaphore_wait(present.at[other], 1)
            pair(other, me).start()

        @pl.when(partner > me)
        def _():
            pl.semaphore_wait(near.at[2], 1)
            to_partner.start()

        @pl.when(me == 0)
        def _():
            pl.semaphore_wait(near.at[1], 1)
            start(to_left[0] + to_left[1])

    @when(even, me >= tiles // 2)
    def _():
        start(to_left[1])

    @when(jnp.logical_not(early))
    def _():
        answer()

    @when(jnp.logical_not(even), me >= tiles // 2, me < tiles - 1)
    def _():
        start(to_right[1])

    @when(topmost)
    def _():
        start(to_left[0] + to_left[1])

    row = iota((lon_cells, LANES), 0)
    open_east = jnp.where(row == last, 0, jnp.minimum(depth, pltpu.roll(depth, last, 0)))
    open_north = jnp.where(
        lane == LANES - 1, 0, jnp.minimum(depth, pltpu.roll(depth, LANES - 1, 1)))
    source = iota((2 * LANES, 2 * LANES), 0) & (LANES - 1)
    target = iota((2 * LANES, 2 * LANES), 1)
    target = jnp.where(target < LANES, target + 1, target - 1) & (LANES - 1)
    shifts[...] = (source == target).astype(F32).astype(BF16)
    nothing = jnp.zeros((PAD, LANES), F32)
    for side in (0, PAD + planes):
        kappa[side:side + PAD, :] = nothing
        for n in range(count):
            tracer[n, side:side + PAD, :] = nothing
    for i in (5, 4, 1):
        loads[i].wait()

    middle = (levels + 1) // 2
    chunks = levels // GROUP
    rounds = (middle + chunks // 2 - 1) // (chunks // 2)
    open_south = jnp.where(lane == 0, 0, pltpu.roll(open_north, 1, 1))

    def eliminate(k, target, coupling, prior, rest):
        here = thickness[at(k), :]
        partial = here + rest
        scale = 1.0 / (partial + coupling)
        gain = coupling * scale
        gains[at(target), :] = gain
        factor[at(target), :] = prior * scale
        share[at(target), :] = here * scale
        return gain * partial

    def below(k):
        near_by = 0.5 * (thickness[at(k), :] + thickness[at(k + 1), :])
        return jnp.where(depth > k + 1, mixing[at(k), :] / near_by, 0.0)

    def shift(c):
        lines = jnp.concatenate(
            [x for g in range(GROUP) for x in split(c * GROUP + g)], axis=0)
        return jnp.dot(lines, shifts[...], preferred_element_type=F32)

    def face(speed, near_kappa, far_kappa, is_open):
        ahead = jnp.maximum(speed, 0.0) + 0.5 * (near_kappa + far_kappa)
        return jnp.where(is_open, ahead, 0.0), jnp.where(is_open, speed - ahead, 0.0)

    def stencil(k, g, shifted):
        def moved(f, way):
            return shifted[(g * (count + 2) + f) * lon_cells:(g * (count + 2) + f + 1) * lon_cells,
                           way * LANES:(way + 1) * LANES]

        spread = kappa[beside(k), :]
        ea, eb = face(east[at(k), :], spread, kappa[beside(k, 1), :], open_east > k)
        na, nb = face(north[at(k), :], spread, moved(count, 0), open_north > k)
        sa, sb = face(moved(count + 1, 1), moved(count, 1), spread, open_south > k)
        west = pltpu.roll(ea, 1, 0)
        centre = 1.0 - ((ea - pltpu.roll(eb, 1, 0)) + (na - sb))
        for n in range(count):
            values[n, at(k), :] = (
                (centre * tracer[n, beside(k), :] + (sa * moved(n, 1) - nb * moved(n, 0)))
                + (west * tracer[n, beside(k, -1), :] - eb * tracer[n, beside(k, 1), :]))

    def group(c, now, later):
        for g in range(GROUP):
            stencil(c * GROUP + g, g, now)
        if later is not None:
            later[...] = shift(c + 1)

    def inner(c, state):
        over, over_rest, under, under_rest = state
        for r in range(rounds):
            k = c * rounds + r
            coupling = below(k)
            over_rest = eliminate(
                k, jnp.where(k < middle, k, levels), coupling, over, over_rest)
            over = coupling
            k = levels - 1 - k
            coupling = below(k - 1)
            under_rest = eliminate(
                k, jnp.where(k >= middle, k, levels), coupling, under, under_rest)
            under = coupling
        group(2 * c, shifted, shifted_more)
        group(2 * c + 1, shifted_more, shifted)
        return over, over_rest, under, under_rest

    shifted[...] = shift(0)
    lax.fori_loop(0, chunks // 2, inner, (empty,) * 4)
    group(chunks - 1, shifted, None)

    @when(early)
    def _():
        answer()

    mine.wait()

    @pl.loop(1, tiles)
    def _(hop):
        other = lax.rem(me + hop, tiles)
        pair(other, other).wait_recv()

    surface = gathered(received, count, lon_cells)
    thin = 1.0 / thickness[at(0), :]
    for n in range(count):
        values[n, at(0), :] = values[n, at(0), :] + jnp.where(depth > 0, surface[n] * thin, 0.0)

    for each in copies:
        each.wait_send()

    @pl.loop(1, tiles)
    def _(hop):
        other = lax.rem(me + hop, tiles)
        pair(other, other).wait_send()

    for each in edges:
        each.wait()
    for each in to_right[0] + to_right[1] + to_left[0] + to_left[1]:
        each.wait_recv()
    deep = iota((levels, LANES), 0)
    wa, wb = weights(right_in[count + 1, rows, :], right_in[count, rows, :], own[0, count, rows, :],
                     deep < jnp.minimum(right_depth[...], depth[:1]))
    ea, eb = weights(own[1, count + 1, rows, :], own[1, count, rows, :], left_in[count, rows, :],
                     deep < jnp.minimum(left_depth[...], depth[last:]))
    for n in range(count):
        halo[0, n, rows, :] = -(wa * right_in[n, rows, :] + wb * own[0, n, rows, :])
        halo[1, n, rows, :] = ea * own[1, n, rows, :] + eb * left_in[n, rows, :]
    to_partner.wait_recv()
    came = [fold_in[n] for n in range(count)]
    kappa_far, north_far = [
        jnp.where(lane < spare, pltpu.roll(came[2 * f], spare, 1),
                  pltpu.roll(came[2 * f + 1], LANES - levels + spare, 1)) for f in range(2)]
    edge_far = jnp.broadcast_to(came[1][:, LANES - 1:], (lon_cells, LANES))
    fa, fb = weights(0.5 * (top[count + 1] - north_far), top[count], kappa_far,
                     lane < jnp.minimum(top[count + 2], edge_far).astype(I32))
    fold = [fa * top[n] + fb * came[n] for n in range(count)]
    half = lon_cells // 2
    line = iota((half, LANES), 0)

    def sweep(k, value):
        part = share[at(k), :]
        mult = factor[at(k), :]
        solved = []
        for n in range(count):
            sides = jnp.concatenate(
                [jnp.where(line == 0, halo[0, n, pl.ds(k, 1), :], 0.0),
                 jnp.where(line == half - 1, halo[1, n, pl.ds(k, 1), :], 0.0)], axis=0)
            across = jnp.where(lane == LANES - 1, pltpu.roll(fold[n], LANES - 1 - k, 1), 0.0)
            solved.append(part * (values[n, at(k), :] - (across + sides)) + mult * value[n])
            values[n, at(k), :] = solved[n]
        return tuple(solved)

    def both(k, state):
        return sweep(k, state[:count]) + sweep(levels - 1 - k, state[count:])

    state = lax.fori_loop(0, levels // 2, both, (empty,) * (2 * count), unroll=5)
    if levels % 2:
        sweep(levels // 2, state[:count])


def finish(lon_cells, values, gains, out, solved, sems):
    count, planes = values.shape[:2]
    levels = planes // lon_cells
    middle = (levels + 1) // 2

    def at(k):
        return pl.ds(pl.multiple_of(k * lon_cells, lon_cells), lon_cells)

    stores = []

    def store(begin, end):
        block = pl.ds(begin * lon_cells, (end - begin) * lon_cells)
        stores.append(pltpu.make_async_copy(
            solved.at[:, block], out.at[:, block], sems.at[len(stores)]))
        stores[-1].start()

    def put(k, value):
        for n in range(count):
            solved[n, at(k), :] = value[n]

    gain, other = gains[at(middle - 1), :], gains[at(middle), :]
    over = [values[n, at(middle - 1), :] for n in range(count)]
    under = [values[n, at(middle), :] for n in range(count)]
    scale = 1.0 / (1.0 - gain * other)
    over = [(a + gain * b) * scale for a, b in zip(over, under)]
    under = [b + other * a for a, b in zip(over, under)]
    put(middle - 1, over)
    put(middle, under)

    top, bottom = middle - 1, middle + 1
    while top > 0 or bottom < levels:
        size = CHUNK - 1 if not stores else CHUNK
        for k in range(top - 1, max(top - size, 0) - 1, -1):
            gain = gains[at(k), :]
            over = [values[n, at(k), :] + gain * over[n] for n in range(count)]
            put(k, over)
        for k in range(bottom, min(bottom + size, levels)):
            gain = gains[at(k), :]
            under = [values[n, at(k), :] + gain * under[n] for n in range(count)]
            put(k, under)
        low, high = max(top - size, 0), min(bottom + size, levels)
        if not stores:
            store(low, high)
        else:
            if low < top:
                store(low, top)
            if bottom < high:
                store(bottom, high)
        top, bottom = low, high
    for each in stores:
        each.wait()


def shards(tracer, east_speed, north_speed, diffusivity, mixing, thickness, depth_levels,
           air_flux, margin_tile, margin_source, margin_cell, margin_weight):
    count, lon_cells, levels, lat_cells = tracer.shape
    tiles = lax.axis_size("lon")
    records = margin_source.shape[0]
    assert lat_cells == LANES and levels < LANES and levels // GROUP % 2 and levels % GROUP == 0 and levels % BATCH == 0

    def by_level(x):
        return x.transpose(1, 0, 2).reshape(levels * lon_cells, LANES)

    operands = (
        tracer.transpose(0, 2, 1, 3).reshape(count, levels * lon_cells, LANES),
        *[by_level(x) for x in (east_speed, north_speed, diffusivity, mixing, thickness)],
        depth_levels, air_flux,
        *[x.reshape(1, records) for x in (margin_tile, margin_source, margin_cell, margin_weight)])
    wide = (
        tracer.transpose(0, 2, 1, 3).reshape(count, levels, lon_cells, 1, LANES),
        *[x.transpose(1, 0, 2).reshape(levels, lon_cells, 1, LANES)
          for x in (diffusivity, east_speed)],
        depth_levels.reshape(lon_cells, 1, LANES))
    held = [pltpu.VMEM(x.shape, x.dtype) for x in operands]
    held[0] = pltpu.VMEM((count, levels * lon_cells + 2 * PAD, LANES), F32)
    held[3] = pltpu.VMEM((levels * lon_cells + 2 * PAD, LANES), F32)
    hbm = pl.BlockSpec(memory_space=pltpu.HBM)
    more = pltpu.VMEM(((levels + 1) * lon_cells, LANES), F32)
    rows = (levels + 7) // 8 * 8
    pairs = pltpu.VMEM((tiles, (count // 2 + 4) // 4 * 4, LANES), F32)
    moved = pltpu.VMEM((GROUP * (count + 2) * lon_cells, 2 * LANES), F32)
    dma = pltpu.SemaphoreType.DMA
    regular = pltpu.SemaphoreType.REGULAR
    vmem = pl.BlockSpec(memory_space=pltpu.VMEM)
    values, gains = pl.pallas_call(
        lambda *refs: step(tiles, *refs),
        out_shape=(pltpu.VMEM(operands[0].shape, F32), more),
        in_specs=[hbm] * 16, out_specs=(vmem, vmem),
        scratch_shapes=held + [
            more, more,
            pltpu.VMEM((count + 3, lon_cells, LANES), F32),
            pltpu.VMEM((count, lon_cells, LANES), F32), pltpu.VMEM((count, lon_cells, LANES), F32),
            pltpu.VMEM((count + 2, rows, LANES), F32), pltpu.VMEM((count + 1, rows, LANES), F32),
            pltpu.VMEM((1, LANES), I32), pltpu.VMEM((1, LANES), I32),
            pltpu.VMEM((2, count + 2, rows, LANES), F32),
            pltpu.VMEM((2, count, rows, LANES), F32),
            pltpu.VMEM((2 * LANES, 2 * LANES), BF16),
            moved, moved, pairs, pairs, dma((24,)), dma((12,)), dma((12,)),
            dma((tiles,)), dma((tiles,)), dma, dma((6,)), regular((3,)), regular((tiles,))],
        compiler_params=pltpu.CompilerParams(
            collective_id=0, has_side_effects=True, vmem_limit_bytes=32 << 20),
        name="ocean_step",
    )(*[pltpu.with_memory_space_constraint(x, pltpu.HBM) for x in operands + wide])
    result = pl.pallas_call(
        lambda *refs: finish(lon_cells, *refs),
        out_shape=pltpu.HBM(values.shape, F32),
        in_specs=[vmem, vmem], out_specs=hbm,
        scratch_shapes=[pltpu.VMEM(values.shape, F32), dma((2 * pl.cdiv(levels, 2 * CHUNK),))],
        name="finish",
    )(*[pltpu.with_memory_space_constraint(x, pltpu.VMEM) for x in (values, gains)])
    return result.reshape(count, levels, lon_cells, LANES).transpose(0, 2, 1, 3)


def solution(mesh):
    placed = (
        P(None, "lon", None, "ens"),
        P("lon", None, "ens"),
        P("lon", None, "ens"),
        P("lon", None, "ens"),
        P("lon", None, "ens"),
        P("lon", None, "ens"),
        P("lon", "ens"),
        P("ens", "lon"),
        P(("ens", "lon"), None),
        P(("ens", "lon")),
        P(("ens", "lon")),
        P(("ens", "lon")),
    )
    return jax.shard_map(
        shards, mesh=mesh, in_specs=placed, out_specs=P(None, "lon", None, "ens"), check_vma=False
    )
```
